256 devices in a mesh: wide: 64 (over x, y, z_lo, core), narrow: 4 (over z_hi).
Axes of the slice: x: 4, y: 4, z: 8 (z_hi: 4, z_lo: 2; z = z_hi * 2 + z_lo), core: 2. Of those that a mesh axis runs over, the one named last changes fastest.
Arguments:
- volume: bfloat16 [64, 128, 32, 512], P(None, 'wide', 'narrow'), may hold values from -6 to 6
- out_grad: bfloat16 [64, 128, 32, 512], P(None, 'wide', 'narrow'), may hold values from -6 to 6
- plane_kernel: bfloat16 [9, 64, 64], replicated, may hold values from -0.25 to 0.25
- z_axis_kernel: bfloat16 [7, 64, 64], replicated, may hold values from -0.25 to 0.25
Outputs:
- volume_grad: bfloat16 [64, 128, 32, 512], P(None, 'wide', 'narrow')
- plane_kernel_grad: float32 [9, 64, 64], replicated
- z_axis_kernel_gradient: float32 [7, 64, 64], replicated
The draws below stay inside these ranges and needn't reach their ends.
All inputs are finite; a program needn't handle non-finite values.
Results may differ from the reference program's by a relative error of at most 0.0061.
Values may be sent and summed in bfloat16 or wider, within the bound.
No kernel may reach another device: no remote copies, remote signals or barrier semaphores. Data moves between devices by JAX's collectives and lax.ppermute only.
A program may use at most 192 MiB of HBM per device.

```python
import math
import jax
import jax.numpy as jnp

CH = 64
YB = 512
Z_DILATION = 4
NZ = 128
NX = 32


def block_scale(key, shape, shards, low, high):
    level, own = 1.0, jax.random.fold_in(key, 6)
    for position, shards_of in shards:
        heights = jnp.exp(jax.random.uniform(jax.random.fold_in(own, position), (shards_of,), jnp.float32, low / len(shards), high / len(shards)))
        level = level * jnp.repeat(heights, shape[position] // shards_of).reshape([-1 if axis == position else 1 for axis in range(len(shape))])
    return level


def gaussian(key, shape, scale, limit, split=(), kind=jnp.bfloat16):
    loudness = block_scale(key, shape, split, -0.22, 0.18) if split else 1.0
    array = jax.random.normal(key, shape, jnp.float32) * scale * loudness
    return jnp.minimum(jnp.maximum(array, -limit), limit).astype(kind)


def setup_inputs(seed: int = 0) -> dict:
    key_of = jax.random.split(jax.random.key(seed), 5)
    return {
        "volume": gaussian(key_of[0], (CH, NZ, NX, YB), 1.0, 6.0, ((1, 64), (2, 4))),
        "out_grad": gaussian(key_of[1], (CH, NZ, NX, YB), 1.0, 6.0, ((1, 64), (2, 4))),
        "plane_kernel": gaussian(key_of[2], (9, CH, CH), (9 * CH) ** -0.5, 0.25),
        "z_axis_kernel": gaussian(key_of[3], (7, CH, CH), (7 * CH) ** -0.5, 0.25),
    }


def silu_slope(values):
    sigmoid = jax.nn.sigmoid(values)
    return sigmoid * (1.0 + values * (1.0 - sigmoid))

def channel_mixing(weight, source):
    width = source.shape[0]
    mixed = jnp.dot(weight, source.reshape(width, -1), preferred_element_type=jnp.float32)
    return mixed.reshape((weight.shape[0],) + source.shape[1:])

def kernel_product(left, right):
    return jnp.dot(left.reshape(left.shape[0], -1), right.reshape(right.shape[0], -1).T, preferred_element_type=jnp.float32)

def plane_slice(padded, kernel_tap_index, rows, cols):
    row_shift = kernel_tap_index // 3
    col_shift = kernel_tap_index % 3
    return padded[:, :, row_shift:row_shift + rows, col_shift:col_shift + cols]

def depth_window(padded, start, depth_axis_size):
    return padded[:, start:start + depth_axis_size]

def reference(volume, out_grad, plane_kernel, z_axis_kernel):
    depth_axis_size = volume.shape[1]
    rows = volume.shape[2]
    cols = volume.shape[3]
    kernel_extent = 3 * Z_DILATION
    padded = jnp.pad(volume, ((0, 0), (0, 0), (1, 1), (1, 1)))
    pre_act = jnp.zeros(volume.shape, jnp.float32)
    for kernel_tap_index in range(9):
        pre_act = pre_act + channel_mixing(plane_kernel[kernel_tap_index], plane_slice(padded, kernel_tap_index, rows, cols))
    acts = jax.nn.silu(pre_act).astype(jnp.bfloat16)
    activation_padded = jnp.pad(acts, ((0, 0), (kernel_extent, kernel_extent), (0, 0), (0, 0)))
    depth_output = jnp.zeros(volume.shape, jnp.float32)
    for kernel_tap_index in range(7):
        depth_output = depth_output + channel_mixing(z_axis_kernel[kernel_tap_index], depth_window(activation_padded, kernel_tap_index * Z_DILATION, depth_axis_size))
    depth_gradient = (out_grad.astype(jnp.float32) * silu_slope(depth_output)).astype(jnp.bfloat16)
    gradient_scale = 1.0 / math.sqrt(depth_axis_size * rows * cols)
    z_axis_kernel_gradient = jnp.stack([kernel_product(depth_gradient, depth_window(activation_padded, kernel_tap_index * Z_DILATION, depth_axis_size)) for kernel_tap_index in range(7)]) * gradient_scale
    gradient_padded = jnp.pad(depth_gradient, ((0, 0), (kernel_extent, kernel_extent), (0, 0), (0, 0)))
    activation_gradient = jnp.zeros(volume.shape, jnp.float32)
    for kernel_tap_index in range(7):
        activation_gradient = activation_gradient + channel_mixing(z_axis_kernel[kernel_tap_index].T, depth_window(gradient_padded, (6 - kernel_tap_index) * Z_DILATION, depth_axis_size))
    activation_gradient = activation_gradient.astype(jnp.bfloat16)
    pre_grad = (activation_gradient.astype(jnp.float32) * silu_slope(pre_act)).astype(jnp.bfloat16)
    plane_kernel_grad = jnp.stack([kernel_product(pre_grad, plane_slice(padded, kernel_tap_index, rows, cols)) for kernel_tap_index in range(9)]) * gradient_scale
    pre_pad = jnp.pad(pre_grad, ((0, 0), (0, 0), (1, 1), (1, 1)))
    volume_grad = out_grad.astype(jnp.float32)
    for kernel_tap_index in range(9):
        volume_grad = volume_grad + channel_mixing(plane_kernel[kernel_tap_index].T, plane_slice(pre_pad, 8 - kernel_tap_index, rows, cols))
    return (volume_grad.astype(jnp.bfloat16), plane_kernel_grad, z_axis_kernel_gradient)
```

```python
import functools
import math

import jax
import jax.numpy as jnp
from jax import lax
from jax.experimental import pallas as pl
from jax.experimental.pallas import tpu as pltpu
from jax.sharding import Mesh
from jax.sharding import PartitionSpec as P

LANES = 128
SPREAD = ("wide_0", "wide_1", "wide_2")
WIDE = SPREAD + ("wide_3",)
FLAT = ("wide_0", "wide_1")
TALL = ("wide_2", "wide_3", "narrow")
FACTORS = (4, 4, 2, 2)


def group_size(axes):
    return math.prod(lax.axis_size(a) for a in axes)


def halo_rows(first, last, axis):
    count = lax.axis_size(axis)
    forward = [(i, i + 1) for i in range(count - 1)]
    backward = [(i + 1, i) for i in range(count - 1)]
    return lax.ppermute(last, axis, forward), lax.ppermute(first, axis, backward)


def sigmoid(v):
    return 1.0 / (1.0 + jnp.exp(-v))


def shifted(block, step):
    width = block.shape[1]
    lane = lax.broadcasted_iota(jnp.int32, block.shape, 1)
    edge = 0 if step == 1 else width - 1
    return jnp.where(lane == edge, 0.0, pltpu.roll(block, step % width, 1))


def fill_rows(rows_ref, vol_ref, low_ref, high_ref):
    slabs, rows, width, cols = vol_ref.shape
    for z in range(slabs):
        rows_ref[z, 0:width, :] = low_ref[z]
        rows_ref[z, (rows + 1) * width :, :] = high_ref[z]

        def copy(x, carry, z=z):
            rows_ref[z, pl.ds(pl.multiple_of((x + 1) * width, width), width), :] = vol_ref[z, x]
            return carry

        lax.fori_loop(0, rows, copy, 0)


def plane_forward_kernel(vol_ref, low_ref, high_ref, w_ref, act_ref, slope_ref, rows_ref):
    slabs, rows, width, cols = vol_ref.shape
    tiles = cols // LANES
    fill_rows(rows_ref, vol_ref, low_ref, high_ref)

    def step(n, carry):
        z, x = n // rows, n % rows
        window = rows_ref[z, pl.ds(pl.multiple_of(x * width, width), 3 * width), :]
        parts = jnp.dot(w_ref[...], window, preferred_element_type=jnp.float32)
        pre = (
            parts[width : 2 * width]
            + shifted(parts[:width], 1)
            + shifted(parts[2 * width :], -1)
        )
        gate = sigmoid(pre)
        slope_ref[z, x] = gate * (1.0 + pre * (1.0 - gate))
        act = (pre * gate).astype(jnp.bfloat16)
        for b in range(tiles):
            act_ref[x * tiles + b, z] = act[:, b * LANES : (b + 1) * LANES]
        return carry

    lax.fori_loop(0, slabs * rows, step, 0)


def depth_kernel(act_ref, grad_ref, wf_ref, wb_ref, out_ref, dw_ref, a_ref, d_ref, acc_ref):
    count, slabs, width, lanes = act_ref.shape
    rim = 3 * width
    cols = slabs * lanes
    zeros = jnp.zeros((rim, cols), jnp.bfloat16)
    for ref in (a_ref, d_ref):
        ref[0:rim, :] = zeros
        ref[rim + count * width :, :] = zeros
    acc_ref[...] = jnp.zeros_like(acc_ref)

    def fill(z, carry):
        for s in range(slabs):
            a_ref[
                pl.ds(pl.multiple_of(rim + z * width, width), width), s * lanes : (s + 1) * lanes
            ] = act_ref[z, s]
        return carry

    lax.fori_loop(0, count, fill, 0)

    def forward(n, carry):
        base = pl.multiple_of(n * 2 * width, 2 * width)
        window = a_ref[pl.ds(base, 8 * width), :]
        depth = jnp.dot(wf_ref[...], window, preferred_element_type=jnp.float32)
        gate = sigmoid(depth)
        slope = gate * (1.0 + depth * (1.0 - gate))
        for a in range(2):
            for s in range(slabs):
                part = slope[a * width : (a + 1) * width, s * lanes : (s + 1) * lanes]
                grad = grad_ref[2 * n + a, s].astype(jnp.float32) * part
                at = pl.multiple_of(rim + base + a * width, width)
                d_ref[pl.ds(at, width), s * lanes : (s + 1) * lanes] = grad.astype(jnp.bfloat16)
        return carry

    lax.fori_loop(0, count // 2, forward, 0)

    def backward(n, carry):
        base = pl.multiple_of(n * 2 * width, 2 * width)
        back = jnp.dot(
            wb_ref[...], d_ref[pl.ds(base, 8 * width), :], preferred_element_type=jnp.float32
        ).astype(jnp.bfloat16)
        for a in range(2):
            for s in range(slabs):
                out_ref[2 * n + a, s] = back[
                    a * width : (a + 1) * width, s * lanes : (s + 1) * lanes
                ]
        acc_ref[...] += lax.dot_general(
            d_ref[pl.ds(pl.multiple_of(rim + base, width), 2 * width), :],
            a_ref[pl.ds(base, 8 * width), :],
            (((1,), (1,)), ((), ())),
            preferred_element_type=jnp.float32,
        )
        return carry

    lax.fori_loop(0, count // 2, backward, 0)
    dw_ref[...] = acc_ref[0:width, :] + pltpu.roll(acc_ref[width:, :], 7 * width, 1)


def plane_grad_kernel(back_ref, slope_ref, rows_ref, dwz_ref, pre_ref, dw_ref, acc_ref):
    slabs, rows, width, cols = slope_ref.shape
    tiles = cols // LANES
    acc_ref[...] = jnp.zeros_like(acc_ref)

    def step(n, carry):
        z, x = n // rows, n % rows
        back = jnp.concatenate([back_ref[x * tiles + b, z] for b in range(tiles)], axis=1)
        grad = (back.astype(jnp.float32) * slope_ref[z, x]).astype(jnp.bfloat16)
        pre_ref[z, x] = grad
        wide = grad.astype(jnp.float32)
        stack = jnp.concatenate(
            [shifted(wide, -1).astype(jnp.bfloat16), grad, shifted(wide, 1).astype(jnp.bfloat16)],
            axis=0,
        )
        window = rows_ref[z, pl.ds(pl.multiple_of(x * width, width), 3 * width), :]
        acc_ref[...] += lax.dot_general(
            stack, window, (((1,), (1,)), ((), ())), preferred_element_type=jnp.float32
        )
        return carry

    lax.fori_loop(0, slabs * rows, step, 0)
    taps = [
        acc_ref[j * width : (j + 1) * width, i * width : (i + 1) * width]
        for i in range(3)
        for j in range(3)
    ] + [dwz_ref[:, k * width : (k + 1) * width] for k in range(7)]
    for p in range(8):
        dw_ref[p] = jnp.concatenate([taps[p], taps[p + 8]], axis=1)


def plane_backward_kernel(pre_ref, low_ref, high_ref, grad_ref, w_ref, out_ref, rows_ref):
    slabs, rows, width, cols = pre_ref.shape
    tiles = cols // LANES
    fill_rows(rows_ref, pre_ref, low_ref, high_ref)

    def step(n, carry):
        z, x = n // rows, n % rows
        window = rows_ref[z, pl.ds(pl.multiple_of(x * width, width), 3 * width), :]
        parts = jnp.dot(w_ref[...], window, preferred_element_type=jnp.float32)
        total = (
            parts[width : 2 * width]
            + shifted(parts[:width], -1)
            + shifted(parts[2 * width :], 1)
        )
        for b in range(tiles):
            lanes = slice(b * LANES, (b + 1) * LANES)
            grad = grad_ref[x * tiles + b, z].astype(jnp.float32)
            out_ref[z, x, :, lanes] = (total[:, lanes] + grad).astype(jnp.bfloat16)
        return carry

    lax.fori_loop(0, slabs * rows, step, 0)


def unpack_kernel(scale, total_ref, plane_ref, depth_ref):
    half = total_ref.shape[2] // 2
    for p in range(8):
        block = total_ref[p] * scale
        plane_ref[p] = block[:, :half]
        if p == 0:
            plane_ref[8] = block[:, half:]
        else:
            depth_ref[p - 1] = block[:, half:]


def call(kernel, name, outs, scratch=(), flops=0):
    vmem = pl.BlockSpec(memory_space=pltpu.VMEM)

    def run(*args):
        moved = sum(a.size * a.dtype.itemsize for a in (*args, *outs))
        return pl.pallas_call(
            kernel,
            out_shape=outs,
            in_specs=[vmem] * len(args),
            out_specs=[vmem] * len(outs),
            scratch_shapes=list(scratch),
            compiler_params=pltpu.CompilerParams(vmem_limit_bytes=40 << 20),
            cost_estimate=pl.CostEstimate(flops=flops, bytes_accessed=moved, transcendentals=0),
            name=name,
        )(*args)

    return run


def group_total(packed):
    first, second = group_size(FLAT), group_size(TALL)
    shape = packed.shape
    pieces = packed.reshape(first, -1, LANES)
    pieces = lax.all_to_all(pieces, FLAT, 0, 0, tiled=True)
    part = jnp.sum(pieces, axis=0)
    copies = jnp.broadcast_to(part[None], (second, *part.shape))
    part = jnp.sum(lax.all_to_all(copies, TALL, 0, 0, tiled=True), axis=0)
    copies = jnp.broadcast_to(part[None], (first, *part.shape))
    return lax.all_to_all(copies, FLAT, 0, 0, tiled=True).reshape(shape)


def on_device(volume, out_grad, plane_kernel, z_axis_kernel):
    width, slabs, rows, cols = volume.shape
    tiles = cols // LANES
    peers = group_size(SPREAD)
    shape = jax.ShapeDtypeStruct
    bf16, f32 = jnp.bfloat16, jnp.float32
    gradient_scale = 1.0 / math.sqrt(
        slabs * group_size(WIDE) * rows * lax.axis_size("narrow") * cols
    )
    blocks = (rows * tiles, slabs, width, LANES)

    grad_blocks = out_grad.reshape(width, slabs, rows, tiles, LANES)
    grad_blocks = grad_blocks.transpose(2, 3, 1, 0, 4).reshape(blocks)
    grad_pencil = lax.all_to_all(grad_blocks, SPREAD, 0, 0, tiled=True)

    taps = plane_kernel.reshape(3, 3, width, width)
    plane_forward = taps.transpose(1, 2, 0, 3).reshape(3 * width, 3 * width)
    plane_backward = taps[::-1].transpose(1, 3, 0, 2).reshape(3 * width, 3 * width)
    none = jnp.zeros((1, width, width), bf16)

    def banded(tap_list):
        upper = jnp.concatenate([tap_list, none]).transpose(1, 0, 2).reshape(width, -1)
        lower = jnp.concatenate([none, tap_list]).transpose(1, 0, 2).reshape(width, -1)
        return jnp.concatenate([upper, lower])

    depth_forward = banded(z_axis_kernel)
    depth_backward = banded(z_axis_kernel[::-1].transpose(0, 2, 1))

    slab = volume.transpose(1, 2, 0, 3)
    low, high = halo_rows(slab[:, 0], slab[:, rows - 1], "narrow")
    plane_flops = 2 * 9 * width * width * slabs * rows * cols
    depth_flops = plane_flops * 7 // 9
    act, slope, rimmed = call(
        plane_forward_kernel,
        "plane_forward",
        (
            shape(blocks, bf16),
            shape((slabs, rows, width, cols), f32),
            shape((slabs, (rows + 2) * width, cols), bf16),
        ),
        flops=plane_flops,
    )(slab, low, high, plane_forward)

    act_pencil = lax.all_to_all(act, SPREAD, 0, 0, tiled=True)
    span = (peers + 6) * width
    back_pencil, depth_term = call(
        depth_kernel,
        "depth",
        (shape(act_pencil.shape, bf16), shape((width, 8 * width), f32)),
        (
            pltpu.VMEM((span, slabs * LANES), bf16),
            pltpu.VMEM((span, slabs * LANES), bf16),
            pltpu.VMEM((2 * width, 8 * width), f32),
        ),
        flops=3 * depth_flops,
    )(act_pencil, grad_pencil, depth_forward, depth_backward)
    back = lax.all_to_all(back_pencil, SPREAD, 0, 0, tiled=True)

    pre_grad, packed = call(
        plane_grad_kernel,
        "plane_grad",
        (shape((slabs, rows, width, cols), bf16), shape((8, width, 2 * width), f32)),
        (pltpu.VMEM((3 * width, 3 * width), f32),),
        flops=plane_flops,
    )(back, slope, rimmed, depth_term)
    low, high = halo_rows(pre_grad[:, 0], pre_grad[:, rows - 1], "narrow")
    total = group_total(packed)
    (volume_grad,) = call(
        plane_backward_kernel,
        "plane_backward",
        (shape((slabs, rows, width, cols), bf16),),
        (pltpu.VMEM((slabs, (rows + 2) * width, cols), bf16),),
        flops=plane_flops,
    )(pre_grad, low, high, grad_blocks, plane_backward)
    plane_total, depth_total = call(
        functools.partial(unpack_kernel, gradient_scale),
        "unpack",
        (shape((9, width, width), f32), shape((7, width, width), f32)),
    )(total)
    return volume_grad.transpose(2, 0, 1, 3), plane_total, depth_total


def solution(mesh):
    names = WIDE + ("narrow",)
    finer = Mesh(mesh.devices.reshape(*FACTORS, mesh.shape["narrow"]), names)
    return jax.shard_map(
        on_device,
        mesh=finer,
        in_specs=(P(None, WIDE, "narrow", None), P(None, WIDE, "narrow", None), P(), P()),
        out_specs=(P(None, WIDE, "narrow", None), P(), P()),
        check_vma=False,
    )
```

```python
import functools
import math

import jax
import jax.numpy as jnp
from jax import lax
from jax.experimental import pallas as pl
from jax.experimental.pallas import tpu as pltpu
from jax.sharding import Mesh
from jax.sharding import PartitionSpec as P

LANES = 128
UNROLL = 8
SPREAD = ("wide_0", "wide_1", "wide_2")
WIDE = SPREAD + ("wide_3",)
FLAT = ("wide_0", "wide_1")
TALL = ("wide_2", "wide_3", "narrow")
FACTORS = (4, 4, 2, 2)


def group_size(axes):
    return math.prod(lax.axis_size(a) for a in axes)


def halo_rows(first, last, axis):
    count = lax.axis_size(axis)
    forward = [(i, i + 1) for i in range(count - 1)]
    backward = [(i + 1, i) for i in range(count - 1)]
    return lax.ppermute(last, axis, forward), lax.ppermute(first, axis, backward)


def sigmoid(v):
    return 1.0 / (1.0 + jnp.exp(-v))


def shifted(block, step):
    width = block.shape[1]
    lane = lax.broadcasted_iota(jnp.int32, block.shape, 1)
    edge = 0 if step == 1 else width - 1
    return jnp.where(lane == edge, 0.0, pltpu.roll(block, step % width, 1))


def fill_rows(rows_ref, vol_ref, low_ref, high_ref):
    slabs, rows, width, _ = vol_ref.shape
    for z in range(slabs):
        rows_ref[z, 0:width, :] = low_ref[z]
        rows_ref[z, (rows + 1) * width :, :] = high_ref[z]

        def copy(x, carry, z=z):
            rows_ref[z, pl.ds(pl.multiple_of((x + 1) * width, width), width), :] = vol_ref[z, x]
            return carry

        lax.fori_loop(0, rows, copy, 0, unroll=True)


def plane_forward_kernel(
    vol_ref, low_ref, high_ref, w_ref, grad_ref, both_ref, slope_ref, rows_ref
):
    slabs, rows, width, cols = vol_ref.shape
    tiles = cols // LANES
    fill_rows(rows_ref, vol_ref, low_ref, high_ref)

    def step(n, carry):
        z, x = n // rows, n % rows
        window = rows_ref[z, pl.ds(pl.multiple_of(x * width, width), 3 * width), :]
        parts = jnp.dot(w_ref[...], window, preferred_element_type=jnp.float32)
        pre = (
            parts[width : 2 * width]
            + shifted(parts[:width], 1)
            + shifted(parts[2 * width :], -1)
        )
        gate = sigmoid(pre)
        slope_ref[z, x] = gate * (1.0 + pre * (1.0 - gate))
        act = (pre * gate).astype(jnp.bfloat16)
        for b in range(tiles):
            both_ref[x * tiles + b, z] = act[:, b * LANES : (b + 1) * LANES]
            both_ref[x * tiles + b, slabs + z] = grad_ref[x * tiles + b, z]
        return carry

    lax.fori_loop(0, slabs * rows, step, 0, unroll=UNROLL)


def depth_kernel(both_ref, wf_ref, wb_ref, out_ref, dw_ref, a_ref, d_ref, acc_ref):
    count, slabs, width, lanes = out_ref.shape
    rim = 3 * width
    cols = slabs * lanes
    zeros = jnp.zeros((rim, cols), jnp.bfloat16)
    for ref in (a_ref, d_ref):
        ref[0:rim, :] = zeros
        ref[rim + count * width :, :] = zeros
    acc_ref[...] = jnp.zeros_like(acc_ref)

    def fill(z, carry):
        for s in range(slabs):
            a_ref[
                pl.ds(pl.multiple_of(rim + z * width, width), width), s * lanes : (s + 1) * lanes
            ] = both_ref[z, s]
        return carry

    lax.fori_loop(0, count, fill, 0, unroll=4)

    def forward(n, carry):
        base = pl.multiple_of(n * 2 * width, 2 * width)
        window = a_ref[pl.ds(base, 8 * width), :]
        depth = jnp.dot(wf_ref[...], window, preferred_element_type=jnp.float32)
        gate = sigmoid(depth)
        slope = gate * (1.0 + depth * (1.0 - gate))
        for a in range(2):
            for s in range(slabs):
                part = slope[a * width : (a + 1) * width, s * lanes : (s + 1) * lanes]
                grad = both_ref[2 * n + a, slabs + s].astype(jnp.float32) * part
                at = pl.multiple_of(rim + base + a * width, width)
                d_ref[pl.ds(at, width), s * lanes : (s + 1) * lanes] = grad.astype(jnp.bfloat16)
        return carry

    lax.fori_loop(0, count // 2, forward, 0, unroll=UNROLL)

    def backward(n, carry):
        base = pl.multiple_of(n * 2 * width, 2 * width)
        back = jnp.dot(
            wb_ref[...], d_ref[pl.ds(base, 8 * width), :], preferred_element_type=jnp.float32
        ).astype(jnp.bfloat16)
        for a in range(2):
            for s in range(slabs):
                out_ref[2 * n + a, s] = back[
                    a * width : (a + 1) * width, s * lanes : (s + 1) * lanes
                ]
        acc_ref[...] += lax.dot_general(
            d_ref[pl.ds(pl.multiple_of(rim + base, width), 2 * width), :],
            a_ref[pl.ds(base, 8 * width), :],
            (((1,), (1,)), ((), ())),
            preferred_element_type=jnp.float32,
        )
        return carry

    lax.fori_loop(0, count // 2, backward, 0, unroll=UNROLL)
    dw_ref[...] = acc_ref[0:width, :] + pltpu.roll(acc_ref[width:, :], 7 * width, 1)


def plane_grad_kernel(back_ref, slope_ref, rows_ref, dwz_ref, pre_ref, dw_ref, acc_ref):
    slabs, rows, width, cols = slope_ref.shape
    tiles = cols // LANES
    acc_ref[...] = jnp.zeros_like(acc_ref)

    def step(n, carry):
        z, x = n // rows, n % rows
        back = jnp.concatenate([back_ref[x * tiles + b, z] for b in range(tiles)], axis=1)
        grad = (back.astype(jnp.float32) * slope_ref[z, x]).astype(jnp.bfloat16)
        pre_ref[z, x] = grad
        wide = grad.astype(jnp.float32)
        stack = jnp.concatenate(
            [shifted(wide, -1).astype(jnp.bfloat16), grad, shifted(wide, 1).astype(jnp.bfloat16)],
            axis=0,
        )
        window = rows_ref[z, pl.ds(pl.multiple_of(x * width, width), 3 * width), :]
        acc_ref[...] += lax.dot_general(
            stack, window, (((1,), (1,)), ((), ())), preferred_element_type=jnp.float32
        )
        return carry

    lax.fori_loop(0, slabs * rows, step, 0, unroll=UNROLL)
    taps = [
        acc_ref[j * width : (j + 1) * width, i * width : (i + 1) * width]
        for i in range(3)
        for j in range(3)
    ] + [dwz_ref[:, k * width : (k + 1) * width] for k in range(7)]
    for p in range(8):
        dw_ref[p] = jnp.concatenate([taps[p], taps[p + 8]], axis=1)


def plane_backward_kernel(pre_ref, low_ref, high_ref, grad_ref, w_ref, out_ref, rows_ref):
    slabs, rows, width, cols = pre_ref.shape
    tiles = cols // LANES
    fill_rows(rows_ref, pre_ref, low_ref, high_ref)

    def step(n, carry):
        z, x = n // rows, n % rows
        window = rows_ref[z, pl.ds(pl.multiple_of(x * width, width), 3 * width), :]
        parts = jnp.dot(w_ref[...], window, preferred_element_type=jnp.float32)
        total = (
            parts[width : 2 * width]
            + shifted(parts[:width], -1)
            + shifted(parts[2 * width :], 1)
        )
        for b in range(tiles):
            lanes = slice(b * LANES, (b + 1) * LANES)
            grad = grad_ref[x * tiles + b, z].astype(jnp.float32)
            out_ref[z, x, :, lanes] = (total[:, lanes] + grad).astype(jnp.bfloat16)
        return carry

    lax.fori_loop(0, slabs * rows, step, 0, unroll=UNROLL)


def unpack_kernel(scale, total_ref, plane_ref, depth_ref):
    half = total_ref.shape[2] // 2
    for p in range(8):
        block = total_ref[p] * scale
        plane_ref[p] = block[:, :half]
        if p == 0:
            plane_ref[8] = block[:, half:]
        else:
            depth_ref[p - 1] = block[:, half:]


def call(kernel, outs, scratch=(), flops=0):
    vmem = pl.BlockSpec(memory_space=pltpu.VMEM)

    def run(*args):
        moved = sum(a.size * a.dtype.itemsize for a in (*args, *outs))
        return pl.pallas_call(
            kernel,
            out_shape=outs,
            in_specs=[vmem] * len(args),
            out_specs=[vmem] * len(outs),
            scratch_shapes=list(scratch),
            compiler_params=pltpu.CompilerParams(vmem_limit_bytes=16 << 20),
            cost_estimate=pl.CostEstimate(flops=flops, bytes_accessed=moved, transcendentals=0),
        )(*args)

    return run


def spread_pieces(packed):
    pieces = packed.reshape(group_size(FLAT), -1, LANES)
    return lax.all_to_all(pieces, FLAT, 0, 0, tiled=True)


def copies_of(pieces, count):
    part = jnp.sum(pieces, axis=0)
    return jnp.broadcast_to(part[None], (count, *part.shape))


def on_device(volume, out_grad, plane_kernel, z_axis_kernel):
    width, slabs, rows, cols = volume.shape
    tiles = cols // LANES
    peers = group_size(SPREAD)
    shape = jax.ShapeDtypeStruct
    bf16, f32 = jnp.bfloat16, jnp.float32
    gradient_scale = 1.0 / math.sqrt(
        slabs * group_size(WIDE) * rows * lax.axis_size("narrow") * cols
    )
    blocks = (rows * tiles, slabs, width, LANES)

    slab = volume.transpose(1, 2, 0, 3)
    first, last = slab[:, 0], slab[:, rows - 1]
    low, high = halo_rows(first, last, "narrow")


    grad_blocks = out_grad.reshape(width, slabs, rows, tiles, LANES)
    grad_blocks = grad_blocks.transpose(2, 3, 1, 0, 4).reshape(blocks)

    taps = plane_kernel.reshape(3, 3, width, width)
    plane_forward = taps.transpose(1, 2, 0, 3).reshape(3 * width, 3 * width)
    plane_backward = taps[::-1].transpose(1, 3, 0, 2).reshape(3 * width, 3 * width)
    none = jnp.zeros((1, width, width), bf16)

    def banded(tap_list):
        upper = jnp.concatenate([tap_list, none]).transpose(1, 0, 2).reshape(width, -1)
        lower = jnp.concatenate([none, tap_list]).transpose(1, 0, 2).reshape(width, -1)
        return jnp.concatenate([upper, lower])

    depth_forward = banded(z_axis_kernel)
    depth_backward = banded(z_axis_kernel[::-1].transpose(0, 2, 1))

    plane_flops = 2 * 9 * width * width * slabs * rows * cols
    depth_flops = plane_flops * 7 // 9
    low, high, plane_forward, depth_forward, depth_backward = lax.optimization_barrier(
        (low, high, plane_forward, depth_forward, depth_backward)
    )
    both, slope, rimmed = call(
        plane_forward_kernel,
        (
            shape((blocks[0], 2 * slabs, width, LANES), bf16),
            shape((slabs, rows, width, cols), f32),
            shape((slabs, (rows + 2) * width, cols), bf16),
        ),
        flops=plane_flops,
    )(slab, low, high, plane_forward, grad_blocks)

    both = lax.all_to_all(both, SPREAD, 0, 0, tiled=True)
    span = (peers + 6) * width
    back_pencil, depth_term = call(
        depth_kernel,
        (shape(blocks, bf16), shape((width, 8 * width), f32)),
        (
            pltpu.VMEM((span, slabs * LANES), bf16),
            pltpu.VMEM((span, slabs * LANES), bf16),
            pltpu.VMEM((2 * width, 8 * width), f32),
        ),
        flops=3 * depth_flops,
    )(both, depth_forward, depth_backward)
    back = lax.all_to_all(back_pencil, SPREAD, 0, 0, tiled=True)

    pre_grad, packed = call(
        plane_grad_kernel,
        (shape((slabs, rows, width, cols), bf16), shape((8, width, 2 * width), f32)),
        (pltpu.VMEM((3 * width, 3 * width), f32),),
        flops=plane_flops,
    )(back, slope, rimmed, depth_term)
    low, high = halo_rows(pre_grad[:, 0], pre_grad[:, rows - 1], "narrow")
    pieces = spread_pieces(packed)
    pieces, plane_backward = lax.optimization_barrier((pieces, plane_backward))
    pieces = lax.all_to_all(copies_of(pieces, group_size(TALL)), TALL, 0, 0, tiled=True)
    (volume_grad,) = call(
        plane_backward_kernel,
        (shape((slabs, rows, width, cols), bf16),),
        (pltpu.VMEM((slabs, (rows + 2) * width, cols), bf16),),
        flops=plane_flops,
    )(pre_grad, low, high, grad_blocks, plane_backward)
    volume_grad = volume_grad.transpose(2, 0, 1, 3)
    pieces, volume_grad = lax.optimization_barrier((pieces, volume_grad))
    total = lax.all_to_all(copies_of(pieces, group_size(FLAT)), FLAT, 0, 0, tiled=True)
    plane_total, depth_total = call(
        functools.partial(unpack_kernel, gradient_scale),
        (shape((9, width, width), f32), shape((7, width, width), f32)),
    )(total.reshape(packed.shape))
    return volume_grad, plane_total, depth_total


def solution(mesh):
    names = WIDE + ("narrow",)
    finer = Mesh(mesh.devices.reshape(*FACTORS, mesh.shape["narrow"]), names)
    return jax.shard_map(
        on_device,
        mesh=finer,
        in_specs=(P(None, WIDE, "narrow", None), P(None, WIDE, "narrow", None), P(), P()),
        out_specs=(P(None, WIDE, "narrow", None), P(), P()),
        check_vma=False,
    )
```

```python
import functools
import math

import jax
import jax.numpy as jnp
from jax import lax
from jax.experimental import pallas as pl
from jax.experimental.pallas import tpu as pltpu
from jax.sharding import Mesh
from jax.sharding import PartitionSpec as P

LANES = 128
UNROLL = 8
SPREAD = ("wide_0", "wide_1", "wide_2")
WIDE = SPREAD + ("wide_3",)
FLAT = ("wide_0", "wide_1")
TALL = ("wide_2", "wide_3", "narrow")
FACTORS = (4, 4, 2, 2)


def group_size(axes):
    return math.prod(lax.axis_size(a) for a in axes)


def halo_rows(first, last, axis):
    count = lax.axis_size(axis)
    forward = [(i, i + 1) for i in range(count - 1)]
    backward = [(i + 1, i) for i in range(count - 1)]
    return lax.ppermute(last, axis, forward), lax.ppermute(first, axis, backward)


def sigmoid(v):
    return 1.0 / (1.0 + jnp.exp(-v))


def shifted(block, step):
    width = block.shape[1]
    lane = lax.broadcasted_iota(jnp.int32, block.shape, 1)
    edge = 0 if step == 1 else width - 1
    return jnp.where(lane == edge, 0.0, pltpu.roll(block, step % width, 1))


def fill_rows(rows_ref, vol_ref, low_ref, high_ref):
    slabs, rows, width, _ = vol_ref.shape
    for z in range(slabs):
        rows_ref[z, 0:width, :] = low_ref[z]
        rows_ref[z, (rows + 1) * width :, :] = high_ref[z]

        def copy(x, carry, z=z):
            rows_ref[z, pl.ds(pl.multiple_of((x + 1) * width, width), width), :] = vol_ref[z, x]
            return carry

        lax.fori_loop(0, rows, copy, 0, unroll=True)


def plane_forward_kernel(
    vol_ref, low_ref, high_ref, w_ref, grad_ref, both_ref, slope_ref, rows_ref
):
    slabs, rows, width, cols = vol_ref.shape
    tiles = cols // LANES
    fill_rows(rows_ref, vol_ref, low_ref, high_ref)

    def step(n, carry):
        z, x = n // rows, n % rows
        window = rows_ref[z, pl.ds(pl.multiple_of(x * width, width), 3 * width), :]
        parts = jnp.dot(w_ref[...], window, preferred_element_type=jnp.float32)
        pre = (
            parts[width : 2 * width]
            + shifted(parts[:width], 1)
            + shifted(parts[2 * width :], -1)
        )
        gate = sigmoid(pre)
        slope_ref[z, x] = gate * (1.0 + pre * (1.0 - gate))
        act = (pre * gate).astype(jnp.bfloat16)
        for b in range(tiles):
            both_ref[x * tiles + b, z] = act[:, b * LANES : (b + 1) * LANES]
            both_ref[x * tiles + b, slabs + z] = grad_ref[x * tiles + b, z]
        return carry

    lax.fori_loop(0, slabs * rows, step, 0, unroll=UNROLL)


def depth_kernel(both_ref, wf_ref, wb_ref, out_ref, dw_ref, a_ref, d_ref, acc_ref):
    count, slabs, width, lanes = out_ref.shape
    rim = 3 * width
    cols = slabs * lanes
    zeros = jnp.zeros((rim, cols), jnp.bfloat16)
    for ref in (a_ref, d_ref):
        ref[0:rim, :] = zeros
        ref[rim + count * width :, :] = zeros
    acc_ref[...] = jnp.zeros_like(acc_ref)

    def fill(z, carry):
        for s in range(slabs):
            a_ref[
                pl.ds(pl.multiple_of(rim + z * width, width), width), s * lanes : (s + 1) * lanes
            ] = both_ref[z, s]
        return carry

    lax.fori_loop(0, count, fill, 0, unroll=4)

    def forward(n, carry):
        base = pl.multiple_of(n * 2 * width, 2 * width)
        window = a_ref[pl.ds(base, 8 * width), :]
        depth = jnp.dot(wf_ref[...], window, preferred_element_type=jnp.float32)
        gate = sigmoid(depth)
        slope = gate * (1.0 + depth * (1.0 - gate))
        for a in range(2):
            for s in range(slabs):
                part = slope[a * width : (a + 1) * width, s * lanes : (s + 1) * lanes]
                grad = both_ref[2 * n + a, slabs + s].astype(jnp.float32) * part
                at = pl.multiple_of(rim + base + a * width, width)
                d_ref[pl.ds(at, width), s * lanes : (s + 1) * lanes] = grad.astype(jnp.bfloat16)
        return carry

    lax.fori_loop(0, count // 2, forward, 0, unroll=UNROLL)

    def backward(n, carry):
        base = pl.multiple_of(n * 2 * width, 2 * width)
        back = jnp.dot(
            wb_ref[...], d_ref[pl.ds(base, 8 * width), :], preferred_element_type=jnp.float32
        ).astype(jnp.bfloat16)
        for a in range(2):
            for s in range(slabs):
                out_ref[2 * n + a, s] = back[
                    a * width : (a + 1) * width, s * lanes : (s + 1) * lanes
                ]
        acc_ref[...] += lax.dot_general(
            d_ref[pl.ds(pl.multiple_of(rim + base, width), 2 * width), :],
            a_ref[pl.ds(base, 8 * width), :],
            (((1,), (1,)), ((), ())),
            preferred_element_type=jnp.float32,
        )
        return carry

    lax.fori_loop(0, count // 2, backward, 0, unroll=UNROLL)
    dw_ref[...] = acc_ref[0:width, :] + pltpu.roll(acc_ref[width:, :], 7 * width, 1)


def plane_grad_kernel(back_ref, slope_ref, rows_ref, dwz_ref, pre_ref, dw_ref, acc_ref):
    slabs, rows, width, cols = slope_ref.shape
    tiles = cols // LANES
    acc_ref[...] = jnp.zeros_like(acc_ref)

    def step(n, carry):
        z, x = n // rows, n % rows
        back = jnp.concatenate([back_ref[x * tiles + b, z] for b in range(tiles)], axis=1)
        grad = (back.astype(jnp.float32) * slope_ref[z, x]).astype(jnp.bfloat16)
        pre_ref[z, x] = grad
        wide = grad.astype(jnp.float32)
        stack = jnp.concatenate(
            [shifted(wide, -1).astype(jnp.bfloat16), grad, shifted(wide, 1).astype(jnp.bfloat16)],
            axis=0,
        )
        window = rows_ref[z, pl.ds(pl.multiple_of(x * width, width), 3 * width), :]
        acc_ref[...] += lax.dot_general(
            stack, window, (((1,), (1,)), ((), ())), preferred_element_type=jnp.float32
        )
        return carry

    lax.fori_loop(0, slabs * rows, step, 0, unroll=UNROLL)
    taps = [
        acc_ref[j * width : (j + 1) * width, i * width : (i + 1) * width]
        for i in range(3)
        for j in range(3)
    ] + [dwz_ref[:, k * width : (k + 1) * width] for k in range(7)]
    for p in range(8):
        dw_ref[p] = jnp.concatenate([taps[p], taps[p + 8]], axis=1)


def plane_backward_kernel(pre_ref, low_ref, high_ref, grad_ref, w_ref, out_ref, rows_ref):
    slabs, rows, width, cols = pre_ref.shape
    tiles = cols // LANES
    fill_rows(rows_ref, pre_ref, low_ref, high_ref)

    def step(n, carry):
        z, x = n // rows, n % rows
        window = rows_ref[z, pl.ds(pl.multiple_of(x * width, width), 3 * width), :]
        parts = jnp.dot(w_ref[...], window, preferred_element_type=jnp.float32)
        total = (
            parts[width : 2 * width]
            + shifted(parts[:width], -1)
            + shifted(parts[2 * width :], 1)
        )
        for b in range(tiles):
            lanes = slice(b * LANES, (b + 1) * LANES)
            grad = grad_ref[x * tiles + b, z].astype(jnp.float32)
            out_ref[z, x, :, lanes] = (total[:, lanes] + grad).astype(jnp.bfloat16)
        return carry

    lax.fori_loop(0, slabs * rows, step, 0, unroll=UNROLL)


def unpack_kernel(scale, total_ref, plane_ref, depth_ref):
    half = total_ref.shape[2] // 2
    for p in range(8):
        block = total_ref[p] * scale
        plane_ref[p] = block[:, :half]
        if p == 0:
            plane_ref[8] = block[:, half:]
        else:
            depth_ref[p - 1] = block[:, half:]


def call(kernel, outs, scratch=(), flops=0):
    vmem = pl.BlockSpec(memory_space=pltpu.VMEM)

    def run(*args):
        moved = sum(a.size * a.dtype.itemsize for a in (*args, *outs))
        return pl.pallas_call(
            kernel,
            out_shape=outs,
            in_specs=[vmem] * len(args),
            out_specs=[vmem] * len(outs),
            scratch_shapes=list(scratch),
            compiler_params=pltpu.CompilerParams(vmem_limit_bytes=16 << 20),
            cost_estimate=pl.CostEstimate(flops=flops, bytes_accessed=moved, transcendentals=0),
        )(*args)

    return run


def copies_kernel(pieces_ref, copies_ref):
    part = pieces_ref[0]
    for i in range(1, pieces_ref.shape[0]):
        part = part + pieces_ref[i]
    for i in range(copies_ref.shape[0]):
        copies_ref[i] = part


def spread_pieces(packed):
    pieces = packed.reshape(group_size(TALL), -1, LANES)
    return lax.all_to_all(pieces, TALL, 0, 0, tiled=True)


def copies_of(pieces, count):
    shape = jax.ShapeDtypeStruct((count, *pieces.shape[1:]), pieces.dtype)
    return call(copies_kernel, (shape,))(pieces)[0]


def on_device(volume, out_grad, plane_kernel, z_axis_kernel):
    width, slabs, rows, cols = volume.shape
    tiles = cols // LANES
    peers = group_size(SPREAD)
    shape = jax.ShapeDtypeStruct
    bf16, f32 = jnp.bfloat16, jnp.float32
    gradient_scale = 1.0 / math.sqrt(
        slabs * group_size(WIDE) * rows * lax.axis_size("narrow") * cols
    )
    blocks = (rows * tiles, slabs, width, LANES)

    slab = volume.transpose(1, 2, 0, 3)
    first, last = slab[:, 0], slab[:, rows - 1]
    low, high = halo_rows(first, last, "narrow")


    grad_blocks = out_grad.reshape(width, slabs, rows, tiles, LANES)
    grad_blocks = grad_blocks.transpose(2, 3, 1, 0, 4).reshape(blocks)

    taps = plane_kernel.reshape(3, 3, width, width)
    plane_forward = taps.transpose(1, 2, 0, 3).reshape(3 * width, 3 * width)
    plane_backward = taps[::-1].transpose(1, 3, 0, 2).reshape(3 * width, 3 * width)
    none = jnp.zeros((1, width, width), bf16)

    def banded(tap_list):
        upper = jnp.concatenate([tap_list, none]).transpose(1, 0, 2).reshape(width, -1)
        lower = jnp.concatenate([none, tap_list]).transpose(1, 0, 2).reshape(width, -1)
        return jnp.concatenate([upper, lower])

    depth_forward = banded(z_axis_kernel)
    depth_backward = banded(z_axis_kernel[::-1].transpose(0, 2, 1))

    plane_flops = 2 * 9 * width * width * slabs * rows * cols
    depth_flops = plane_flops * 7 // 9
    low, high, plane_forward, depth_forward, depth_backward = lax.optimization_barrier(
        (low, high, plane_forward, depth_forward, depth_backward)
    )
    both, slope, rimmed = call(
        plane_forward_kernel,
        (
            shape((blocks[0], 2 * slabs, width, LANES), bf16),
            shape((slabs, rows, width, cols), f32),
            shape((slabs, (rows + 2) * width, cols), bf16),
        ),
        flops=plane_flops,
    )(slab, low, high, plane_forward, grad_blocks)

    both = lax.all_to_all(both, SPREAD, 0, 0, tiled=True)
    span = (peers + 6) * width
    back_pencil, depth_term = call(
        depth_kernel,
        (shape(blocks, bf16), shape((width, 8 * width), f32)),
        (
            pltpu.VMEM((span, slabs * LANES), bf16),
            pltpu.VMEM((span, slabs * LANES), bf16),
            pltpu.VMEM((2 * width, 8 * width), f32),
        ),
        flops=3 * depth_flops,
    )(both, depth_forward, depth_backward)
    back = lax.all_to_all(back_pencil, SPREAD, 0, 0, tiled=True)

    pre_grad, packed = call(
        plane_grad_kernel,
        (shape((slabs, rows, width, cols), bf16), shape((8, width, 2 * width), f32)),
        (pltpu.VMEM((3 * width, 3 * width), f32),),
        flops=plane_flops,
    )(back, slope, rimmed, depth_term)
    low, high = halo_rows(pre_grad[:, 0], pre_grad[:, rows - 1], "narrow")
    pieces = spread_pieces(packed)
    pieces = lax.all_to_all(copies_of(pieces, group_size(FLAT)), FLAT, 0, 0, tiled=True)
    pieces, plane_backward = lax.optimization_barrier((pieces, plane_backward))
    (volume_grad,) = call(
        plane_backward_kernel,
        (shape((slabs, rows, width, cols), bf16),),
        (pltpu.VMEM((slabs, (rows + 2) * width, cols), bf16),),
        flops=plane_flops,
    )(pre_grad, low, high, grad_blocks, plane_backward)
    volume_grad = volume_grad.transpose(2, 0, 1, 3)
    total = lax.all_to_all(copies_of(pieces, group_size(TALL)), TALL, 0, 0, tiled=True)
    plane_total, depth_total = call(
        functools.partial(unpack_kernel, gradient_scale),
        (shape((9, width, width), f32), shape((7, width, width), f32)),
    )(total.reshape(packed.shape))
    return volume_grad, plane_total, depth_total


def solution(mesh):
    names = WIDE + ("narrow",)
    finer = Mesh(mesh.devices.reshape(*FACTORS, mesh.shape["narrow"]), names)
    return jax.shard_map(
        on_device,
        mesh=finer,
        in_specs=(P(None, WIDE, "narrow", None), P(None, WIDE, "narrow", None), P(), P()),
        out_specs=(P(None, WIDE, "narrow", None), P(), P()),
        check_vma=False,
    )
```

```python
import functools
import math

import jax
import jax.numpy as jnp
from jax import lax
from jax.experimental import pallas as pl
from jax.experimental.pallas import tpu as pltpu
from jax.sharding import Mesh
from jax.sharding import PartitionSpec as P

LANES = 128
UNROLL = 16
SPREAD = ("wide_0", "wide_2", "wide_1")
WIDE = ("wide_0", "wide_1", "wide_2", "wide_3")
FLAT = ("wide_0", "wide_1")
TALL = ("wide_2", "wide_3", "narrow")
FACTORS = (4, 4, 2, 2)


def group_size(axes):
    return math.prod(lax.axis_size(a) for a in axes)


def halo_rows(first, last, axis):
    count = lax.axis_size(axis)
    forward = [(i, i + 1) for i in range(count - 1)]
    backward = [(i + 1, i) for i in range(count - 1)]
    return lax.ppermute(last, axis, forward), lax.ppermute(first, axis, backward)


def sigmoid(v):
    return 1.0 / (1.0 + jnp.exp(-v))


def shifted(block, step):
    width = block.shape[1]
    lane = lax.broadcasted_iota(jnp.int32, block.shape, 1)
    edge = 0 if step == 1 else width - 1
    return jnp.where(lane == edge, 0.0, pltpu.roll(block, step % width, 1))


def fill_rows(rows_ref, vol_ref, low_ref, high_ref):
    rows, slabs, width, _ = vol_ref.shape
    for z in range(slabs):
        rows_ref[z, 0:width, :] = low_ref[z]
        rows_ref[z, (rows + 1) * width :, :] = high_ref[z]

        def copy(x, carry, z=z):
            rows_ref[z, pl.ds(pl.multiple_of((x + 1) * width, width), width), :] = vol_ref[x, z]
            return carry

        lax.fori_loop(0, rows, copy, 0, unroll=True)


def plane_forward_kernel(
    vol_ref, low_ref, high_ref, w_ref, grad_ref, both_ref, slope_ref, rows_ref
):
    rows, slabs, width, cols = vol_ref.shape
    tiles = cols // LANES
    fill_rows(rows_ref, vol_ref, low_ref, high_ref)

    def step(n, carry):
        z, x = n // rows, n % rows
        window = rows_ref[z, pl.ds(pl.multiple_of(x * width, width), 3 * width), :]
        parts = jnp.dot(w_ref[...], window, preferred_element_type=jnp.float32)
        pre = (
            parts[width : 2 * width]
            + shifted(parts[:width], 1)
            + shifted(parts[2 * width :], -1)
        )
        gate = sigmoid(pre)
        slope_ref[z, x] = gate * (1.0 + pre * (1.0 - gate))
        act = (pre * gate).astype(jnp.bfloat16)
        for b in range(tiles):
            both_ref[x * tiles + b, z] = act[:, b * LANES : (b + 1) * LANES]
            both_ref[x * tiles + b, slabs + z] = grad_ref[x * tiles + b, z]
        return carry

    lax.fori_loop(0, slabs * rows, step, 0, unroll=UNROLL)


def peer_of(position, inner, outer):
    z, rest = position % inner, position // inner
    return (rest // outer) * (inner * outer) + z * outer + rest % outer


def depth_kernel(inner, outer, both_ref, wf_ref, wb_ref, out_ref, dw_ref, a_ref, d_ref, acc_ref):
    count, slabs, width, lanes = out_ref.shape
    rim = 3 * width
    cols = slabs * lanes
    zeros = jnp.zeros((rim, cols), jnp.bfloat16)
    for ref in (a_ref, d_ref):
        ref[0:rim, :] = zeros
        ref[rim + count * width :, :] = zeros
    acc_ref[...] = jnp.zeros_like(acc_ref)

    def fill(z, carry):
        for s in range(slabs):
            a_ref[
                pl.ds(pl.multiple_of(rim + z * width, width), width), s * lanes : (s + 1) * lanes
            ] = both_ref[peer_of(z, inner, outer), s]
        return carry

    lax.fori_loop(0, count, fill, 0, unroll=4)

    def forward(n, carry):
        base = pl.multiple_of(n * 2 * width, 2 * width)
        window = a_ref[pl.ds(base, 8 * width), :]
        depth = jnp.dot(wf_ref[...], window, preferred_element_type=jnp.float32)
        gate = sigmoid(depth)
        slope = gate * (1.0 + depth * (1.0 - gate))
        for a in range(2):
            for s in range(slabs):
                part = slope[a * width : (a + 1) * width, s * lanes : (s + 1) * lanes]
                grad = both_ref[peer_of(2 * n + a, inner, outer), slabs + s].astype(jnp.float32) * part
                at = pl.multiple_of(rim + base + a * width, width)
                d_ref[pl.ds(at, width), s * lanes : (s + 1) * lanes] = grad.astype(jnp.bfloat16)
        return carry

    lax.fori_loop(0, count // 2, forward, 0, unroll=UNROLL)

    def backward(n, carry):
        base = pl.multiple_of(n * 2 * width, 2 * width)
        back = jnp.dot(
            wb_ref[...], d_ref[pl.ds(base, 8 * width), :], preferred_element_type=jnp.float32
        ).astype(jnp.bfloat16)
        for a in range(2):
            for s in range(slabs):
                out_ref[peer_of(2 * n + a, inner, outer), s] = back[
                    a * width : (a + 1) * width, s * lanes : (s + 1) * lanes
                ]
        acc_ref[...] += lax.dot_general(
            d_ref[pl.ds(pl.multiple_of(rim + base, width), 2 * width), :],
            a_ref[pl.ds(base, 8 * width), :],
            (((1,), (1,)), ((), ())),
            preferred_element_type=jnp.float32,
        )
        return carry

    lax.fori_loop(0, count // 2, backward, 0, unroll=UNROLL)
    dw_ref[...] = acc_ref[0:width, :] + pltpu.roll(acc_ref[width:, :], 7 * width, 1)


def plane_grad_kernel(back_ref, slope_ref, rows_ref, dwz_ref, pre_ref, dw_ref, acc_ref):
    slabs, rows, width, cols = slope_ref.shape
    tiles = cols // LANES
    acc_ref[...] = jnp.zeros_like(acc_ref)

    def step(n, carry):
        z, x = n // rows, n % rows
        back = jnp.concatenate([back_ref[x * tiles + b, z] for b in range(tiles)], axis=1)
        grad = (back.astype(jnp.float32) * slope_ref[z, x]).astype(jnp.bfloat16)
        pre_ref[x, z] = grad
        wide = grad.astype(jnp.float32)
        stack = jnp.concatenate(
            [shifted(wide, -1).astype(jnp.bfloat16), grad, shifted(wide, 1).astype(jnp.bfloat16)],
            axis=0,
        )
        window = rows_ref[z, pl.ds(pl.multiple_of(x * width, width), 3 * width), :]
        acc_ref[...] += lax.dot_general(
            stack, window, (((1,), (1,)), ((), ())), preferred_element_type=jnp.float32
        )
        return carry

    lax.fori_loop(0, slabs * rows, step, 0, unroll=UNROLL)
    taps = [
        acc_ref[j * width : (j + 1) * width, i * width : (i + 1) * width]
        for i in range(3)
        for j in range(3)
    ] + [dwz_ref[:, k * width : (k + 1) * width] for k in range(7)]
    for p in range(8):
        dw_ref[p] = jnp.concatenate([taps[p], taps[p + 8]], axis=1)


def plane_backward_kernel(pre_ref, low_ref, high_ref, grad_ref, w_ref, out_ref, rows_ref):
    rows, slabs, width, cols = pre_ref.shape
    tiles = cols // LANES
    fill_rows(rows_ref, pre_ref, low_ref, high_ref)

    def step(n, carry):
        z, x = n // rows, n % rows
        window = rows_ref[z, pl.ds(pl.multiple_of(x * width, width), 3 * width), :]
        parts = jnp.dot(w_ref[...], window, preferred_element_type=jnp.float32)
        total = (
            parts[width : 2 * width]
            + shifted(parts[:width], -1)
            + shifted(parts[2 * width :], 1)
        )
        for b in range(tiles):
            lanes = slice(b * LANES, (b + 1) * LANES)
            grad = grad_ref[x * tiles + b, z].astype(jnp.float32)
            out_ref[x, z, :, lanes] = (total[:, lanes] + grad).astype(jnp.bfloat16)
        return carry

    lax.fori_loop(0, slabs * rows, step, 0, unroll=UNROLL)


def unpack_kernel(scale, total_ref, plane_ref, depth_ref):
    half = total_ref.shape[2] // 2
    for p in range(8):
        block = total_ref[p] * scale
        plane_ref[p] = block[:, :half]
        if p == 0:
            plane_ref[8] = block[:, half:]
        else:
            depth_ref[p - 1] = block[:, half:]


def call(kernel, outs, scratch=(), flops=0):
    vmem = pl.BlockSpec(memory_space=pltpu.VMEM)

    def run(*args):
        moved = sum(a.size * a.dtype.itemsize for a in (*args, *outs))
        return pl.pallas_call(
            kernel,
            out_shape=outs,
            in_specs=[vmem] * len(args),
            out_specs=[vmem] * len(outs),
            scratch_shapes=list(scratch),
            compiler_params=pltpu.CompilerParams(vmem_limit_bytes=16 << 20),
            cost_estimate=pl.CostEstimate(flops=flops, bytes_accessed=moved, transcendentals=0),
        )(*args)

    return run


def copies_kernel(pieces_ref, copies_ref):
    part = pieces_ref[0]
    for i in range(1, pieces_ref.shape[0]):
        part = part + pieces_ref[i]
    for i in range(copies_ref.shape[0]):
        copies_ref[i] = part


def spread_pieces(packed):
    pieces = packed.reshape(group_size(TALL), -1, LANES)
    return lax.all_to_all(pieces, TALL, 0, 0, tiled=True)


def copies_of(pieces, count):
    shape = jax.ShapeDtypeStruct((count, *pieces.shape[1:]), pieces.dtype)
    return call(copies_kernel, (shape,))(pieces)[0]


def on_device(volume, out_grad, plane_kernel, z_axis_kernel):
    width, slabs, rows, cols = volume.shape
    tiles = cols // LANES
    peers = group_size(SPREAD)
    shape = jax.ShapeDtypeStruct
    bf16, f32 = jnp.bfloat16, jnp.float32
    gradient_scale = 1.0 / math.sqrt(
        slabs * group_size(WIDE) * rows * lax.axis_size("narrow") * cols
    )
    blocks = (rows * tiles, slabs, width, LANES)

    slab = volume.transpose(2, 1, 0, 3)
    first, last = slab[0], slab[rows - 1]
    low, high = halo_rows(first, last, "narrow")


    grad_blocks = out_grad.reshape(width, slabs, rows, tiles, LANES)
    grad_blocks = grad_blocks.transpose(2, 3, 1, 0, 4).reshape(blocks)

    taps = plane_kernel.reshape(3, 3, width, width)
    plane_forward = taps.transpose(1, 2, 0, 3).reshape(3 * width, 3 * width)
    plane_backward = taps[::-1].transpose(1, 3, 0, 2).reshape(3 * width, 3 * width)
    none = jnp.zeros((1, width, width), bf16)

    def banded(tap_list):
        upper = jnp.concatenate([tap_list, none]).transpose(1, 0, 2).reshape(width, -1)
        lower = jnp.concatenate([none, tap_list]).transpose(1, 0, 2).reshape(width, -1)
        return jnp.concatenate([upper, lower])

    depth_forward = banded(z_axis_kernel)
    depth_backward = banded(z_axis_kernel[::-1].transpose(0, 2, 1))

    plane_flops = 2 * 9 * width * width * slabs * rows * cols
    depth_flops = plane_flops * 7 // 9
    low, high, plane_forward, plane_backward, depth_forward, depth_backward = (
        lax.optimization_barrier(
            (low, high, plane_forward, plane_backward, depth_forward, depth_backward)
        )
    )
    both, slope, rimmed = call(
        plane_forward_kernel,
        (
            shape((blocks[0], 2 * slabs, width, LANES), bf16),
            shape((slabs, rows, width, cols), f32),
            shape((slabs, (rows + 2) * width, cols), bf16),
        ),
        flops=plane_flops,
    )(slab, low, high, plane_forward, grad_blocks)

    both = lax.all_to_all(both, SPREAD, 0, 0, tiled=True)
    span = (peers + 6) * width
    back_pencil, depth_term = call(
        functools.partial(depth_kernel, lax.axis_size("wide_2"), lax.axis_size("wide_1")),
        (shape(blocks, bf16), shape((width, 8 * width), f32)),
        (
            pltpu.VMEM((span, slabs * LANES), bf16),
            pltpu.VMEM((span, slabs * LANES), bf16),
            pltpu.VMEM((2 * width, 8 * width), f32),
        ),
        flops=3 * depth_flops,
    )(both, depth_forward, depth_backward)
    back = lax.all_to_all(back_pencil, SPREAD, 0, 0, tiled=True)

    pre_grad, packed = call(
        plane_grad_kernel,
        (shape((rows, slabs, width, cols), bf16), shape((8, width, 2 * width), f32)),
        (pltpu.VMEM((3 * width, 3 * width), f32),),
        flops=plane_flops,
    )(back, slope, rimmed, depth_term)
    low, high = halo_rows(pre_grad[0], pre_grad[rows - 1], "narrow")
    pieces = spread_pieces(packed)
    pieces, plane_backward = lax.optimization_barrier((pieces, plane_backward))
    pieces = lax.all_to_all(copies_of(pieces, group_size(FLAT)), FLAT, 0, 0, tiled=True)
    (volume_grad,) = call(
        plane_backward_kernel,
        (shape((rows, slabs, width, cols), bf16),),
        (pltpu.VMEM((slabs, (rows + 2) * width, cols), bf16),),
        flops=plane_flops,
    )(pre_grad, low, high, grad_blocks, plane_backward)
    volume_grad = volume_grad.transpose(2, 1, 0, 3)
    pieces, volume_grad = lax.optimization_barrier((pieces, volume_grad))
    total = lax.all_to_all(copies_of(pieces, group_size(TALL)), TALL, 0, 0, tiled=True)
    plane_total, depth_total = call(
        functools.partial(unpack_kernel, gradient_scale),
        (shape((9, width, width), f32), shape((7, width, width), f32)),
    )(total.reshape(packed.shape))
    return volume_grad, plane_total, depth_total


def solution(mesh):
    names = WIDE + ("narrow",)
    finer = Mesh(mesh.devices.reshape(*FACTORS, mesh.shape["narrow"]), names)
    return jax.shard_map(
        on_device,
        mesh=finer,
        in_specs=(P(None, WIDE, "narrow", None), P(None, WIDE, "narrow", None), P(), P()),
        out_specs=(P(None, WIDE, "narrow", None), P(), P()),
        check_vma=False,
    )
```

```python
import functools
import math

import jax
import jax.numpy as jnp
from jax import lax
from jax.experimental import pallas as pl
from jax.experimental.pallas import tpu as pltpu
from jax.sharding import Mesh
from jax.sharding import PartitionSpec as P

LANES = 128
UNROLL = 16
SPREAD = ("wide_0", "wide_2", "wide_1")
WIDE = ("wide_0", "wide_1", "wide_2", "wide_3")
FLAT = ("wide_0", "wide_1", "wide_3")
TALL = ("wide_2", "narrow")
FACTORS = (4, 4, 2, 2)


def group_size(axes):
    return math.prod(lax.axis_size(a) for a in axes)


def halo_rows(first, last, axis):
    count = lax.axis_size(axis)
    forward = [(i, i + 1) for i in range(count - 1)]
    backward = [(i + 1, i) for i in range(count - 1)]
    return lax.ppermute(last, axis, forward), lax.ppermute(first, axis, backward)


def sigmoid(v):
    return 1.0 / (1.0 + jnp.exp(-v))


def shifted(block, step):
    width = block.shape[1]
    lane = lax.broadcasted_iota(jnp.int32, block.shape, 1)
    edge = 0 if step == 1 else width - 1
    return jnp.where(lane == edge, 0.0, pltpu.roll(block, step % width, 1))


def fill_rows(rows_ref, vol_ref, low_ref, high_ref):
    rows, slabs, width, _ = vol_ref.shape
    for z in range(slabs):
        rows_ref[z, 0:width, :] = low_ref[z]
        rows_ref[z, (rows + 1) * width :, :] = high_ref[z]

        def copy(x, carry, z=z):
            rows_ref[z, pl.ds(pl.multiple_of((x + 1) * width, width), width), :] = vol_ref[x, z]
            return carry

        lax.fori_loop(0, rows, copy, 0, unroll=True)


def plane_forward_kernel(
    vol_ref, low_ref, high_ref, w_ref, grad_ref, both_ref, slope_ref, rows_ref
):
    rows, slabs, width, cols = vol_ref.shape
    tiles = cols // LANES
    fill_rows(rows_ref, vol_ref, low_ref, high_ref)

    def step(n, carry):
        z, x = n // rows, n % rows
        window = rows_ref[z, pl.ds(pl.multiple_of(x * width, width), 3 * width), :]
        parts = jnp.dot(w_ref[...], window, preferred_element_type=jnp.float32)
        pre = (
            parts[width : 2 * width]
            + shifted(parts[:width], 1)
            + shifted(parts[2 * width :], -1)
        )
        gate = sigmoid(pre)
        slope_ref[z, x] = gate * (1.0 + pre * (1.0 - gate))
        act = (pre * gate).astype(jnp.bfloat16)
        for b in range(tiles):
            both_ref[x * tiles + b, z] = act[:, b * LANES : (b + 1) * LANES]
            both_ref[x * tiles + b, slabs + z] = grad_ref[x * tiles + b, z]
        return carry

    lax.fori_loop(0, slabs * rows, step, 0, unroll=UNROLL)


def peer_of(position, inner, outer):
    z, rest = position % inner, position // inner
    return (rest // outer) * (inner * outer) + z * outer + rest % outer


def depth_kernel(inner, outer, both_ref, wf_ref, wb_ref, out_ref, dw_ref, a_ref, d_ref, acc_ref):
    count, slabs, width, lanes = out_ref.shape
    rim = 3 * width
    cols = slabs * lanes
    zeros = jnp.zeros((rim, cols), jnp.bfloat16)
    for ref in (a_ref, d_ref):
        ref[0:rim, :] = zeros
        ref[rim + count * width :, :] = zeros
    acc_ref[...] = jnp.zeros_like(acc_ref)

    def fill(z, carry):
        for s in range(slabs):
            a_ref[
                pl.ds(pl.multiple_of(rim + z * width, width), width), s * lanes : (s + 1) * lanes
            ] = both_ref[peer_of(z, inner, outer), s]
        return carry

    lax.fori_loop(0, count, fill, 0, unroll=4)

    def forward(n, carry):
        base = pl.multiple_of(n * 2 * width, 2 * width)
        window = a_ref[pl.ds(base, 8 * width), :]
        depth = jnp.dot(wf_ref[...], window, preferred_element_type=jnp.float32)
        gate = sigmoid(depth)
        slope = gate * (1.0 + depth * (1.0 - gate))
        for a in range(2):
            for s in range(slabs):
                part = slope[a * width : (a + 1) * width, s * lanes : (s + 1) * lanes]
                grad = both_ref[peer_of(2 * n + a, inner, outer), slabs + s].astype(jnp.float32) * part
                at = pl.multiple_of(rim + base + a * width, width)
                d_ref[pl.ds(at, width), s * lanes : (s + 1) * lanes] = grad.astype(jnp.bfloat16)
        return carry

    lax.fori_loop(0, count // 2, forward, 0, unroll=UNROLL)

    def backward(n, carry):
        base = pl.multiple_of(n * 2 * width, 2 * width)
        back = jnp.dot(
            wb_ref[...], d_ref[pl.ds(base, 8 * width), :], preferred_element_type=jnp.float32
        ).astype(jnp.bfloat16)
        for a in range(2):
            for s in range(slabs):
                out_ref[peer_of(2 * n + a, inner, outer), s] = back[
                    a * width : (a + 1) * width, s * lanes : (s + 1) * lanes
                ]
        acc_ref[...] += lax.dot_general(
            d_ref[pl.ds(pl.multiple_of(rim + base, width), 2 * width), :],
            a_ref[pl.ds(base, 8 * width), :],
            (((1,), (1,)), ((), ())),
            preferred_element_type=jnp.float32,
        )
        return carry

    lax.fori_loop(0, count // 2, backward, 0, unroll=UNROLL)
    dw_ref[...] = acc_ref[0:width, :] + pltpu.roll(acc_ref[width:, :], 7 * width, 1)


def plane_grad_kernel(back_ref, slope_ref, rows_ref, dwz_ref, pre_ref, dw_ref, acc_ref):
    slabs, rows, width, cols = slope_ref.shape
    tiles = cols // LANES
    acc_ref[...] = jnp.zeros_like(acc_ref)

    def step(n, carry):
        z, x = n // rows, n % rows
        back = jnp.concatenate([back_ref[x * tiles + b, z] for b in range(tiles)], axis=1)
        grad = (back.astype(jnp.float32) * slope_ref[z, x]).astype(jnp.bfloat16)
        pre_ref[x, z] = grad
        wide = grad.astype(jnp.float32)
        stack = jnp.concatenate(
            [shifted(wide, -1).astype(jnp.bfloat16), grad, shifted(wide, 1).astype(jnp.bfloat16)],
            axis=0,
        )
        window = rows_ref[z, pl.ds(pl.multiple_of(x * width, width), 3 * width), :]
        acc_ref[...] += lax.dot_general(
            stack, window, (((1,), (1,)), ((), ())), preferred_element_type=jnp.float32
        )
        return carry

    lax.fori_loop(0, slabs * rows, step, 0, unroll=UNROLL)
    taps = [
        acc_ref[j * width : (j + 1) * width, i * width : (i + 1) * width]
        for i in range(3)
        for j in range(3)
    ] + [dwz_ref[:, k * width : (k + 1) * width] for k in range(7)]
    for p in range(8):
        dw_ref[p] = jnp.concatenate([taps[p], taps[p + 8]], axis=1)


def plane_backward_kernel(pre_ref, low_ref, high_ref, grad_ref, w_ref, out_ref, rows_ref):
    rows, slabs, width, cols = pre_ref.shape
    tiles = cols // LANES
    fill_rows(rows_ref, pre_ref, low_ref, high_ref)

    def step(n, carry):
        z, x = n // rows, n % rows
        window = rows_ref[z, pl.ds(pl.multiple_of(x * width, width), 3 * width), :]
        parts = jnp.dot(w_ref[...], window, preferred_element_type=jnp.float32)
        total = (
            parts[width : 2 * width]
            + shifted(parts[:width], -1)
            + shifted(parts[2 * width :], 1)
        )
        for b in range(tiles):
            lanes = slice(b * LANES, (b + 1) * LANES)
            grad = grad_ref[x * tiles + b, z].astype(jnp.float32)
            out_ref[x, z, :, lanes] = (total[:, lanes] + grad).astype(jnp.bfloat16)
        return carry

    lax.fori_loop(0, slabs * rows, step, 0, unroll=UNROLL)


def unpack_kernel(scale, total_ref, plane_ref, depth_ref):
    half = total_ref.shape[2] // 2
    for p in range(8):
        block = total_ref[p] * scale
        plane_ref[p] = block[:, :half]
        if p == 0:
            plane_ref[8] = block[:, half:]
        else:
            depth_ref[p - 1] = block[:, half:]


def call(kernel, outs, scratch=(), flops=0):
    vmem = pl.BlockSpec(memory_space=pltpu.VMEM)

    def run(*args):
        moved = sum(a.size * a.dtype.itemsize for a in (*args, *outs))
        return pl.pallas_call(
            kernel,
            out_shape=outs,
            in_specs=[vmem] * len(args),
            out_specs=[vmem] * len(outs),
            scratch_shapes=list(scratch),
            compiler_params=pltpu.CompilerParams(vmem_limit_bytes=16 << 20),
            cost_estimate=pl.CostEstimate(flops=flops, bytes_accessed=moved, transcendentals=0),
        )(*args)

    return run


def copies_kernel(pieces_ref, copies_ref):
    part = pieces_ref[0]
    for i in range(1, pieces_ref.shape[0]):
        part = part + pieces_ref[i]
    for i in range(copies_ref.shape[0]):
        copies_ref[i] = part


def spread_pieces(packed):
    pieces = packed.reshape(group_size(FLAT), -1, LANES)
    return lax.all_to_all(pieces, FLAT, 0, 0, tiled=True)


def copies_of(pieces, count):
    shape = jax.ShapeDtypeStruct((count, *pieces.shape[1:]), pieces.dtype)
    return call(copies_kernel, (shape,))(pieces)[0]


def on_device(volume, out_grad, plane_kernel, z_axis_kernel):
    width, slabs, rows, cols = volume.shape
    tiles = cols // LANES
    peers = group_size(SPREAD)
    shape = jax.ShapeDtypeStruct
    bf16, f32 = jnp.bfloat16, jnp.float32
    gradient_scale = 1.0 / math.sqrt(
        slabs * group_size(WIDE) * rows * lax.axis_size("narrow") * cols
    )
    blocks = (rows * tiles, slabs, width, LANES)

    slab = volume.transpose(2, 1, 0, 3)
    first, last = slab[0], slab[rows - 1]
    low, high = halo_rows(first, last, "narrow")


    grad_blocks = out_grad.reshape(width, slabs, rows, tiles, LANES)
    grad_blocks = grad_blocks.transpose(2, 3, 1, 0, 4).reshape(blocks)

    taps = plane_kernel.reshape(3, 3, width, width)
    plane_forward = taps.transpose(1, 2, 0, 3).reshape(3 * width, 3 * width)
    plane_backward = taps[::-1].transpose(1, 3, 0, 2).reshape(3 * width, 3 * width)
    none = jnp.zeros((1, width, width), bf16)

    def banded(tap_list):
        upper = jnp.concatenate([tap_list, none]).transpose(1, 0, 2).reshape(width, -1)
        lower = jnp.concatenate([none, tap_list]).transpose(1, 0, 2).reshape(width, -1)
        return jnp.concatenate([upper, lower])

    depth_forward = banded(z_axis_kernel)
    depth_backward = banded(z_axis_kernel[::-1].transpose(0, 2, 1))

    plane_flops = 2 * 9 * width * width * slabs * rows * cols
    depth_flops = plane_flops * 7 // 9
    low, high, plane_forward, plane_backward, depth_forward, depth_backward = (
        lax.optimization_barrier(
            (low, high, plane_forward, plane_backward, depth_forward, depth_backward)
        )
    )
    both, slope, rimmed = call(
        plane_forward_kernel,
        (
            shape((blocks[0], 2 * slabs, width, LANES), bf16),
            shape((slabs, rows, width, cols), f32),
            shape((slabs, (rows + 2) * width, cols), bf16),
        ),
        flops=plane_flops,
    )(slab, low, high, plane_forward, grad_blocks)

    both = lax.all_to_all(both, SPREAD, 0, 0, tiled=True)
    span = (peers + 6) * width
    back_pencil, depth_term = call(
        functools.partial(depth_kernel, lax.axis_size("wide_2"), lax.axis_size("wide_1")),
        (shape(blocks, bf16), shape((width, 8 * width), f32)),
        (
            pltpu.VMEM((span, slabs * LANES), bf16),
            pltpu.VMEM((span, slabs * LANES), bf16),
            pltpu.VMEM((2 * width, 8 * width), f32),
        ),
        flops=3 * depth_flops,
    )(both, depth_forward, depth_backward)
    back = lax.all_to_all(back_pencil, SPREAD, 0, 0, tiled=True)

    pre_grad, packed = call(
        plane_grad_kernel,
        (shape((rows, slabs, width, cols), bf16), shape((8, width, 2 * width), f32)),
        (pltpu.VMEM((3 * width, 3 * width), f32),),
        flops=plane_flops,
    )(back, slope, rimmed, depth_term)
    low, high = halo_rows(pre_grad[0], pre_grad[rows - 1], "narrow")
    pieces = spread_pieces(packed)
    pieces = lax.all_to_all(copies_of(pieces, group_size(TALL)), TALL, 0, 0, tiled=True)
    pieces, plane_backward = lax.optimization_barrier((pieces, plane_backward))
    (volume_grad,) = call(
        plane_backward_kernel,
        (shape((rows, slabs, width, cols), bf16),),
        (pltpu.VMEM((slabs, (rows + 2) * width, cols), bf16),),
        flops=plane_flops,
    )(pre_grad, low, high, grad_blocks, plane_backward)
    volume_grad = volume_grad.transpose(2, 1, 0, 3)
    total = lax.all_to_all(copies_of(pieces, group_size(FLAT)), FLAT, 0, 0, tiled=True)
    plane_total, depth_total = call(
        functools.partial(unpack_kernel, gradient_scale),
        (shape((9, width, width), f32), shape((7, width, width), f32)),
    )(total.reshape(packed.shape))
    return volume_grad, plane_total, depth_total


def solution(mesh):
    names = WIDE + ("narrow",)
    finer = Mesh(mesh.devices.reshape(*FACTORS, mesh.shape["narrow"]), names)
    return jax.shard_map(
        on_device,
        mesh=finer,
        in_specs=(P(None, WIDE, "narrow", None), P(None, WIDE, "narrow", None), P(), P()),
        out_specs=(P(None, WIDE, "narrow", None), P(), P()),
        check_vma=False,
    )
```

```python
import functools
import math

import jax
import jax.numpy as jnp
from jax import lax
from jax.experimental import pallas as pl
from jax.experimental.pallas import tpu as pltpu
from jax.sharding import Mesh
from jax.sharding import PartitionSpec as P

LANES = 128
UNROLL = 16
SPREAD = ("wide_0", "wide_2", "wide_1")
WIDE = ("wide_0", "wide_1", "wide_2", "wide_3")
FLAT = ("wide_0", "wide_1", "wide_3")
TALL = ("wide_2", "narrow")
FACTORS = (4, 4, 2, 2)


def group_size(axes):
    return math.prod(lax.axis_size(a) for a in axes)


def from_below(last, axis):
    return lax.ppermute(last, axis, [(i, i + 1) for i in range(lax.axis_size(axis) - 1)])


def from_above(first, axis):
    return lax.ppermute(first, axis, [(i + 1, i) for i in range(lax.axis_size(axis) - 1)])


def sigmoid(v):
    return 1.0 / (1.0 + jnp.exp(-v))


def shifted(block, step):
    width = block.shape[1]
    lane = lax.broadcasted_iota(jnp.int32, block.shape, 1)
    edge = 0 if step == 1 else width - 1
    return jnp.where(lane == edge, 0.0, pltpu.roll(block, step % width, 1))


def fill_rows(rows_ref, vol_ref, low_ref, high_ref):
    rows, slabs, width, _ = vol_ref.shape
    for z in range(slabs):
        rows_ref[z, 0:width, :] = low_ref[z]
        rows_ref[z, (rows + 1) * width :, :] = high_ref[z]

        def copy(x, carry, z=z):
            rows_ref[z, pl.ds(pl.multiple_of((x + 1) * width, width), width), :] = vol_ref[x, z]
            return carry

        lax.fori_loop(0, rows, copy, 0, unroll=True)


def plane_forward_kernel(
    vol_ref, low_ref, high_ref, w_ref, grad_ref, both_ref, slope_ref, rows_ref
):
    rows, slabs, width, cols = vol_ref.shape
    tiles = cols // LANES
    fill_rows(rows_ref, vol_ref, low_ref, high_ref)

    def step(n, carry):
        z, x = n // rows, n % rows
        window = rows_ref[z, pl.ds(pl.multiple_of(x * width, width), 3 * width), :]
        parts = jnp.dot(w_ref[...], window, preferred_element_type=jnp.float32)
        pre = (
            parts[width : 2 * width]
            + shifted(parts[:width], 1)
            + shifted(parts[2 * width :], -1)
        )
        gate = sigmoid(pre)
        slope_ref[z, x] = gate * (1.0 + pre * (1.0 - gate))
        act = (pre * gate).astype(jnp.bfloat16)
        for b in range(tiles):
            both_ref[x * tiles + b, z] = act[:, b * LANES : (b + 1) * LANES]
            both_ref[x * tiles + b, slabs + z] = grad_ref[x * tiles + b, z]
        return carry

    lax.fori_loop(0, slabs * rows, step, 0, unroll=UNROLL)


def peer_of(position, inner, outer):
    z, rest = position % inner, position // inner
    return (rest // outer) * (inner * outer) + z * outer + rest % outer


def depth_kernel(inner, outer, both_ref, wf_ref, wb_ref, out_ref, dw_ref, a_ref, d_ref, acc_ref):
    count, slabs, width, lanes = out_ref.shape
    rim = 3 * width
    cols = slabs * lanes
    zeros = jnp.zeros((rim, cols), jnp.bfloat16)
    for ref in (a_ref, d_ref):
        ref[0:rim, :] = zeros
        ref[rim + count * width :, :] = zeros
    acc_ref[...] = jnp.zeros_like(acc_ref)

    def fill(z, carry):
        for s in range(slabs):
            a_ref[
                pl.ds(pl.multiple_of(rim + z * width, width), width), s * lanes : (s + 1) * lanes
            ] = both_ref[peer_of(z, inner, outer), s]
        return carry

    lax.fori_loop(0, count, fill, 0, unroll=4)

    def forward(n, carry):
        base = pl.multiple_of(n * 2 * width, 2 * width)
        window = a_ref[pl.ds(base, 8 * width), :]
        depth = jnp.dot(wf_ref[...], window, preferred_element_type=jnp.float32)
        gate = sigmoid(depth)
        slope = gate * (1.0 + depth * (1.0 - gate))
        for a in range(2):
            for s in range(slabs):
                part = slope[a * width : (a + 1) * width, s * lanes : (s + 1) * lanes]
                grad = both_ref[peer_of(2 * n + a, inner, outer), slabs + s].astype(jnp.float32) * part
                at = pl.multiple_of(rim + base + a * width, width)
                d_ref[pl.ds(at, width), s * lanes : (s + 1) * lanes] = grad.astype(jnp.bfloat16)
        return carry

    lax.fori_loop(0, count // 2, forward, 0, unroll=UNROLL)

    def backward(n, carry):
        base = pl.multiple_of(n * 2 * width, 2 * width)
        back = jnp.dot(
            wb_ref[...], d_ref[pl.ds(base, 8 * width), :], preferred_element_type=jnp.float32
        ).astype(jnp.bfloat16)
        for a in range(2):
            for s in range(slabs):
                out_ref[peer_of(2 * n + a, inner, outer), s] = back[
                    a * width : (a + 1) * width, s * lanes : (s + 1) * lanes
                ]
        acc_ref[...] += lax.dot_general(
            d_ref[pl.ds(pl.multiple_of(rim + base, width), 2 * width), :],
            a_ref[pl.ds(base, 8 * width), :],
            (((1,), (1,)), ((), ())),
            preferred_element_type=jnp.float32,
        )
        return carry

    lax.fori_loop(0, count // 2, backward, 0, unroll=UNROLL)
    dw_ref[...] = acc_ref[0:width, :] + pltpu.roll(acc_ref[width:, :], 7 * width, 1)


def plane_grad_kernel(back_ref, slope_ref, rows_ref, dwz_ref, pre_ref, dw_ref, acc_ref):
    slabs, rows, width, cols = slope_ref.shape
    tiles = cols // LANES
    acc_ref[...] = jnp.zeros_like(acc_ref)

    def step(n, carry):
        z, x = n // rows, n % rows
        back = jnp.concatenate([back_ref[x * tiles + b, z] for b in range(tiles)], axis=1)
        grad = (back.astype(jnp.float32) * slope_ref[z, x]).astype(jnp.bfloat16)
        pre_ref[x, z] = grad
        wide = grad.astype(jnp.float32)
        stack = jnp.concatenate(
            [shifted(wide, -1).astype(jnp.bfloat16), grad, shifted(wide, 1).astype(jnp.bfloat16)],
            axis=0,
        )
        window = rows_ref[z, pl.ds(pl.multiple_of(x * width, width), 3 * width), :]
        acc_ref[...] += lax.dot_general(
            stack, window, (((1,), (1,)), ((), ())), preferred_element_type=jnp.float32
        )
        return carry

    lax.fori_loop(0, slabs * rows, step, 0, unroll=UNROLL)
    taps = [
        acc_ref[j * width : (j + 1) * width, i * width : (i + 1) * width]
        for i in range(3)
        for j in range(3)
    ] + [dwz_ref[:, k * width : (k + 1) * width] for k in range(7)]
    for p in range(8):
        dw_ref[p] = jnp.concatenate([taps[p], taps[p + 8]], axis=1)


def plane_backward_kernel(pre_ref, low_ref, high_ref, grad_ref, w_ref, out_ref, rows_ref):
    rows, slabs, width, cols = pre_ref.shape
    tiles = cols // LANES
    fill_rows(rows_ref, pre_ref, low_ref, high_ref)

    def step(n, carry):
        z, x = n // rows, n % rows
        window = rows_ref[z, pl.ds(pl.multiple_of(x * width, width), 3 * width), :]
        parts = jnp.dot(w_ref[...], window, preferred_element_type=jnp.float32)
        total = (
            parts[width : 2 * width]
            + shifted(parts[:width], -1)
            + shifted(parts[2 * width :], 1)
        )
        for b in range(tiles):
            lanes = slice(b * LANES, (b + 1) * LANES)
            grad = grad_ref[x * tiles + b, z].astype(jnp.float32)
            out_ref[x, z, :, lanes] = (total[:, lanes] + grad).astype(jnp.bfloat16)
        return carry

    lax.fori_loop(0, slabs * rows, step, 0, unroll=UNROLL)


def unpack_kernel(scale, total_ref, plane_ref, depth_ref):
    half = total_ref.shape[2] // 2
    for p in range(8):
        block = total_ref[p] * scale
        plane_ref[p] = block[:, :half]
        if p == 0:
            plane_ref[8] = block[:, half:]
        else:
            depth_ref[p - 1] = block[:, half:]


def call(kernel, outs, scratch=(), flops=0):
    vmem = pl.BlockSpec(memory_space=pltpu.VMEM)

    def run(*args):
        moved = sum(a.size * a.dtype.itemsize for a in (*args, *outs))
        return pl.pallas_call(
            kernel,
            out_shape=outs,
            in_specs=[vmem] * len(args),
            out_specs=[vmem] * len(outs),
            scratch_shapes=list(scratch),
            compiler_params=pltpu.CompilerParams(vmem_limit_bytes=16 << 20),
            cost_estimate=pl.CostEstimate(flops=flops, bytes_accessed=moved, transcendentals=0),
        )(*args)

    return run


def weights_kernel(plane_ref, depth_ref, pf_ref, pb_ref, df_ref, db_ref):
    _, width, _ = plane_ref.shape
    none = jnp.zeros((width, width), jnp.bfloat16)

    def block(row, col):
        return (
            slice(row * width, (row + 1) * width),
            slice(col * width, (col + 1) * width),
        )

    def turned(tap):
        return tap.astype(jnp.float32).T.astype(jnp.bfloat16)

    for i in range(3):
        for j in range(3):
            pf_ref[block(j, i)] = plane_ref[3 * i + j]
            pb_ref[block(j, 2 - i)] = turned(plane_ref[3 * i + j])
    for a in range(2):
        for b in range(8):
            inside = 0 <= b - a < 7
            df_ref[block(a, b)] = depth_ref[b - a] if inside else none
            db_ref[block(a, b)] = turned(depth_ref[6 - (b - a)]) if inside else none


def copies_kernel(pieces_ref, copies_ref):
    part = pieces_ref[0]
    for i in range(1, pieces_ref.shape[0]):
        part = part + pieces_ref[i]
    for i in range(copies_ref.shape[0]):
        copies_ref[i] = part


def spread_pieces(packed):
    pieces = packed.reshape(group_size(FLAT), -1, LANES)
    return lax.all_to_all(pieces, FLAT, 0, 0, tiled=True)


def copies_of(pieces, count):
    shape = jax.ShapeDtypeStruct((count, *pieces.shape[1:]), pieces.dtype)
    return call(copies_kernel, (shape,))(pieces)[0]


def on_device(volume, out_grad, plane_kernel, z_axis_kernel):
    width, slabs, rows, cols = volume.shape
    tiles = cols // LANES
    peers = group_size(SPREAD)
    shape = jax.ShapeDtypeStruct
    bf16, f32 = jnp.bfloat16, jnp.float32
    gradient_scale = 1.0 / math.sqrt(
        slabs * group_size(WIDE) * rows * lax.axis_size("narrow") * cols
    )
    blocks = (rows * tiles, slabs, width, LANES)

    slab = volume.transpose(2, 1, 0, 3)
    first, last = slab[0], slab[rows - 1]
    low, high = from_below(last, "narrow"), from_above(first, "narrow")


    grad_blocks = out_grad.reshape(width, slabs, rows, tiles, LANES)
    grad_blocks = grad_blocks.transpose(2, 3, 1, 0, 4).reshape(blocks)

    plane_forward, plane_backward, depth_forward, depth_backward = call(
        weights_kernel,
        (
            shape((3 * width, 3 * width), bf16),
            shape((3 * width, 3 * width), bf16),
            shape((2 * width, 8 * width), bf16),
            shape((2 * width, 8 * width), bf16),
        ),
    )(plane_kernel, z_axis_kernel)

    plane_flops = 2 * 9 * width * width * slabs * rows * cols
    depth_flops = plane_flops * 7 // 9
    low, high, plane_forward, depth_forward, depth_backward = lax.optimization_barrier(
        (low, high, plane_forward, depth_forward, depth_backward)
    )
    both, slope, rimmed = call(
        plane_forward_kernel,
        (
            shape((blocks[0], 2 * slabs, width, LANES), bf16),
            shape((slabs, rows, width, cols), f32),
            shape((slabs, (rows + 2) * width, cols), bf16),
        ),
        flops=plane_flops,
    )(slab, low, high, plane_forward, grad_blocks)

    both = lax.all_to_all(both, SPREAD, 0, 0, tiled=True)
    span = (peers + 6) * width
    back_pencil, depth_term = call(
        functools.partial(depth_kernel, lax.axis_size("wide_2"), lax.axis_size("wide_1")),
        (shape(blocks, bf16), shape((width, 8 * width), f32)),
        (
            pltpu.VMEM((span, slabs * LANES), bf16),
            pltpu.VMEM((span, slabs * LANES), bf16),
            pltpu.VMEM((2 * width, 8 * width), f32),
        ),
        flops=3 * depth_flops,
    )(both, depth_forward, depth_backward)
    back = lax.all_to_all(back_pencil, SPREAD, 0, 0, tiled=True)

    pre_grad, packed = call(
        plane_grad_kernel,
        (shape((rows, slabs, width, cols), bf16), shape((8, width, 2 * width), f32)),
        (pltpu.VMEM((3 * width, 3 * width), f32),),
        flops=plane_flops,
    )(back, slope, rimmed, depth_term)
    low = from_below(pre_grad[rows - 1], "narrow")
    high = from_above(pre_grad[0], "narrow")
    pieces = spread_pieces(packed)
    pieces = lax.all_to_all(copies_of(pieces, group_size(TALL)), TALL, 0, 0, tiled=True)
    pieces, plane_backward = lax.optimization_barrier((pieces, plane_backward))
    (volume_grad,) = call(
        plane_backward_kernel,
        (shape((rows, slabs, width, cols), bf16),),
        (pltpu.VMEM((slabs, (rows + 2) * width, cols), bf16),),
        flops=plane_flops,
    )(pre_grad, low, high, grad_blocks, plane_backward)
    volume_grad = volume_grad.transpose(2, 1, 0, 3)
    total = lax.all_to_all(copies_of(pieces, group_size(FLAT)), FLAT, 0, 0, tiled=True)
    plane_total, depth_total = call(
        functools.partial(unpack_kernel, gradient_scale),
        (shape((9, width, width), f32), shape((7, width, width), f32)),
    )(total.reshape(packed.shape))
    return volume_grad, plane_total, depth_total


def solution(mesh):
    names = WIDE + ("narrow",)
    finer = Mesh(mesh.devices.reshape(*FACTORS, mesh.shape["narrow"]), names)
    return jax.shard_map(
        on_device,
        mesh=finer,
        in_specs=(P(None, WIDE, "narrow", None), P(None, WIDE, "narrow", None), P(), P()),
        out_specs=(P(None, WIDE, "narrow", None), P(), P()),
        check_vma=False,
    )
```

```python
import functools
import math

import jax
import jax.numpy as jnp
from jax import lax
from jax.experimental import pallas as pl
from jax.experimental.pallas import tpu as pltpu
from jax.sharding import Mesh
from jax.sharding import PartitionSpec as P

LANES = 128
UNROLL = 16
SPREAD = ("wide_2", "wide_0", "wide_1")
WIDE = ("wide_0", "wide_1", "wide_2", "wide_3")
FLAT = ("wide_3", "wide_0", "wide_1")
TALL = ("wide_2", "narrow")
FACTORS = (4, 4, 2, 2)


def group_size(axes):
    return math.prod(lax.axis_size(a) for a in axes)


def from_below(last, axis):
    return lax.ppermute(last, axis, [(i, i + 1) for i in range(lax.axis_size(axis) - 1)])


def from_above(first, axis):
    return lax.ppermute(first, axis, [(i + 1, i) for i in range(lax.axis_size(axis) - 1)])


def sigmoid(v):
    return 1.0 / (1.0 + jnp.exp(-v))


def shifted(block, step):
    width = block.shape[1]
    lane = lax.broadcasted_iota(jnp.int32, block.shape, 1)
    edge = 0 if step == 1 else width - 1
    return jnp.where(lane == edge, 0.0, pltpu.roll(block, step % width, 1))


def fill_rows(rows_ref, vol_ref, low_ref, high_ref):
    rows, slabs, width, _ = vol_ref.shape
    for z in range(slabs):
        rows_ref[z, 0:width, :] = low_ref[z]
        rows_ref[z, (rows + 1) * width :, :] = high_ref[z]

        def copy(x, carry, z=z):
            rows_ref[z, pl.ds(pl.multiple_of((x + 1) * width, width), width), :] = vol_ref[x, z]
            return carry

        lax.fori_loop(0, rows, copy, 0, unroll=True)


def plane_forward_kernel(
    vol_ref, low_ref, high_ref, w_ref, grad_ref, both_ref, slope_ref, rows_ref
):
    rows, slabs, width, cols = vol_ref.shape
    tiles = cols // LANES
    fill_rows(rows_ref, vol_ref, low_ref, high_ref)

    def step(n, carry):
        z, x = n // rows, n % rows
        window = rows_ref[z, pl.ds(pl.multiple_of(x * width, width), 3 * width), :]
        parts = jnp.dot(w_ref[...], window, preferred_element_type=jnp.float32)
        pre = (
            parts[width : 2 * width]
            + shifted(parts[:width], 1)
            + shifted(parts[2 * width :], -1)
        )
        gate = sigmoid(pre)
        slope_ref[z, x] = gate * (1.0 + pre * (1.0 - gate))
        act = (pre * gate).astype(jnp.bfloat16)
        for b in range(tiles):
            both_ref[x * tiles + b, z] = act[:, b * LANES : (b + 1) * LANES]
            both_ref[x * tiles + b, slabs + z] = grad_ref[x * tiles + b, z]
        return carry

    lax.fori_loop(0, slabs * rows, step, 0, unroll=UNROLL)


def peer_of(position, inner, outer):
    return (position % inner) * outer + position // inner


def depth_kernel(inner, outer, both_ref, wf_ref, wb_ref, out_ref, dw_ref, a_ref, d_ref, acc_ref):
    count, slabs, width, lanes = out_ref.shape
    rim = 3 * width
    cols = slabs * lanes
    zeros = jnp.zeros((rim, cols), jnp.bfloat16)
    for ref in (a_ref, d_ref):
        ref[0:rim, :] = zeros
        ref[rim + count * width :, :] = zeros
    acc_ref[...] = jnp.zeros_like(acc_ref)

    def fill(z, carry):
        for s in range(slabs):
            a_ref[
                pl.ds(pl.multiple_of(rim + z * width, width), width), s * lanes : (s + 1) * lanes
            ] = both_ref[peer_of(z, inner, outer), s]
        return carry

    lax.fori_loop(0, count, fill, 0, unroll=4)

    def forward(n, carry):
        base = pl.multiple_of(n * 2 * width, 2 * width)
        window = a_ref[pl.ds(base, 8 * width), :]
        depth = jnp.dot(wf_ref[...], window, preferred_element_type=jnp.float32)
        gate = sigmoid(depth)
        slope = gate * (1.0 + depth * (1.0 - gate))
        for a in range(2):
            for s in range(slabs):
                part = slope[a * width : (a + 1) * width, s * lanes : (s + 1) * lanes]
                grad = both_ref[peer_of(2 * n + a, inner, outer), slabs + s].astype(jnp.float32) * part
                at = pl.multiple_of(rim + base + a * width, width)
                d_ref[pl.ds(at, width), s * lanes : (s + 1) * lanes] = grad.astype(jnp.bfloat16)
        return carry

    lax.fori_loop(0, count // 2, forward, 0, unroll=UNROLL)

    def backward(n, carry):
        base = pl.multiple_of(n * 2 * width, 2 * width)
        back = jnp.dot(
            wb_ref[...], d_ref[pl.ds(base, 8 * width), :], preferred_element_type=jnp.float32
        ).astype(jnp.bfloat16)
        for a in range(2):
            for s in range(slabs):
                out_ref[peer_of(2 * n + a, inner, outer), s] = back[
                    a * width : (a + 1) * width, s * lanes : (s + 1) * lanes
                ]
        acc_ref[...] += lax.dot_general(
            d_ref[pl.ds(pl.multiple_of(rim + base, width), 2 * width), :],
            a_ref[pl.ds(base, 8 * width), :],
            (((1,), (1,)), ((), ())),
            preferred_element_type=jnp.float32,
        )
        return carry

    lax.fori_loop(0, count // 2, backward, 0, unroll=UNROLL)
    dw_ref[...] = acc_ref[0:width, :] + pltpu.roll(acc_ref[width:, :], 7 * width, 1)


def plane_grad_kernel(back_ref, slope_ref, rows_ref, dwz_ref, pre_ref, dw_ref, acc_ref):
    slabs, rows, width, cols = slope_ref.shape
    tiles = cols // LANES
    acc_ref[...] = jnp.zeros_like(acc_ref)

    def step(n, carry):
        z, x = n // rows, n % rows
        back = jnp.concatenate([back_ref[x * tiles + b, z] for b in range(tiles)], axis=1)
        grad = (back.astype(jnp.float32) * slope_ref[z, x]).astype(jnp.bfloat16)
        pre_ref[x, z] = grad
        wide = grad.astype(jnp.float32)
        stack = jnp.concatenate(
            [shifted(wide, -1).astype(jnp.bfloat16), grad, shifted(wide, 1).astype(jnp.bfloat16)],
            axis=0,
        )
        window = rows_ref[z, pl.ds(pl.multiple_of(x * width, width), 3 * width), :]
        acc_ref[...] += lax.dot_general(
            stack, window, (((1,), (1,)), ((), ())), preferred_element_type=jnp.float32
        )
        return carry

    lax.fori_loop(0, slabs * rows, step, 0, unroll=UNROLL)
    taps = [
        acc_ref[j * width : (j + 1) * width, i * width : (i + 1) * width]
        for i in range(3)
        for j in range(3)
    ] + [dwz_ref[:, k * width : (k + 1) * width] for k in range(7)]
    for p in range(8):
        dw_ref[p] = jnp.concatenate([taps[p], taps[p + 8]], axis=1)


def plane_backward_kernel(pre_ref, low_ref, high_ref, grad_ref, w_ref, out_ref, rows_ref):
    rows, slabs, width, cols = pre_ref.shape
    tiles = cols // LANES
    fill_rows(rows_ref, pre_ref, low_ref, high_ref)

    def step(n, carry):
        z, x = n // rows, n % rows
        window = rows_ref[z, pl.ds(pl.multiple_of(x * width, width), 3 * width), :]
        parts = jnp.dot(w_ref[...], window, preferred_element_type=jnp.float32)
        total = (
            parts[width : 2 * width]
            + shifted(parts[:width], -1)
            + shifted(parts[2 * width :], 1)
        )
        for b in range(tiles):
            lanes = slice(b * LANES, (b + 1) * LANES)
            grad = grad_ref[x * tiles + b, z].astype(jnp.float32)
            out_ref[x, z, :, lanes] = (total[:, lanes] + grad).astype(jnp.bfloat16)
        return carry

    lax.fori_loop(0, slabs * rows, step, 0, unroll=UNROLL)


def unpack_kernel(scale, total_ref, plane_ref, depth_ref):
    half = total_ref.shape[2] // 2
    for p in range(8):
        block = total_ref[p] * scale
        plane_ref[p] = block[:, :half]
        if p == 0:
            plane_ref[8] = block[:, half:]
        else:
            depth_ref[p - 1] = block[:, half:]


def call(kernel, outs, scratch=(), flops=0):
    vmem = pl.BlockSpec(memory_space=pltpu.VMEM)

    def run(*args):
        moved = sum(a.size * a.dtype.itemsize for a in (*args, *outs))
        return pl.pallas_call(
            kernel,
            out_shape=outs,
            in_specs=[vmem] * len(args),
            out_specs=[vmem] * len(outs),
            scratch_shapes=list(scratch),
            compiler_params=pltpu.CompilerParams(vmem_limit_bytes=16 << 20),
            cost_estimate=pl.CostEstimate(flops=flops, bytes_accessed=moved, transcendentals=0),
        )(*args)

    return run


def weights_kernel(plane_ref, depth_ref, pf_ref, pb_ref, df_ref, db_ref):
    _, width, _ = plane_ref.shape
    none = jnp.zeros((width, width), jnp.bfloat16)

    def block(row, col):
        return (
            slice(row * width, (row + 1) * width),
            slice(col * width, (col + 1) * width),
        )

    def turned(tap):
        return tap.astype(jnp.float32).T.astype(jnp.bfloat16)

    for i in range(3):
        for j in range(3):
            pf_ref[block(j, i)] = plane_ref[3 * i + j]
            pb_ref[block(j, 2 - i)] = turned(plane_ref[3 * i + j])
    for a in range(2):
        for b in range(8):
            inside = 0 <= b - a < 7
            df_ref[block(a, b)] = depth_ref[b - a] if inside else none
            db_ref[block(a, b)] = turned(depth_ref[6 - (b - a)]) if inside else none


def copies_kernel(pieces_ref, copies_ref):
    part = pieces_ref[0]
    for i in range(1, pieces_ref.shape[0]):
        part = part + pieces_ref[i]
    for i in range(copies_ref.shape[0]):
        copies_ref[i] = part


def spread_pieces(packed):
    pieces = packed.reshape(group_size(FLAT), -1, LANES)
    return lax.all_to_all(pieces, FLAT, 0, 0, tiled=True)


def copies_of(pieces, count):
    shape = jax.ShapeDtypeStruct((count, *pieces.shape[1:]), pieces.dtype)
    return call(copies_kernel, (shape,))(pieces)[0]


def on_device(volume, out_grad, plane_kernel, z_axis_kernel):
    width, slabs, rows, cols = volume.shape
    tiles = cols // LANES
    peers = group_size(SPREAD)
    shape = jax.ShapeDtypeStruct
    bf16, f32 = jnp.bfloat16, jnp.float32
    gradient_scale = 1.0 / math.sqrt(
        slabs * group_size(WIDE) * rows * lax.axis_size("narrow") * cols
    )
    blocks = (rows * tiles, slabs, width, LANES)

    slab = volume.transpose(2, 1, 0, 3)
    first, last = slab[0], slab[rows - 1]
    low, high = from_below(last, "narrow"), from_above(first, "narrow")


    grad_blocks = out_grad.reshape(width, slabs, rows, tiles, LANES)
    grad_blocks = grad_blocks.transpose(2, 3, 1, 0, 4).reshape(blocks)

    plane_forward, plane_backward, depth_forward, depth_backward = call(
        weights_kernel,
        (
            shape((3 * width, 3 * width), bf16),
            shape((3 * width, 3 * width), bf16),
            shape((2 * width, 8 * width), bf16),
            shape((2 * width, 8 * width), bf16),
        ),
    )(plane_kernel, z_axis_kernel)

    plane_flops = 2 * 9 * width * width * slabs * rows * cols
    depth_flops = plane_flops * 7 // 9
    low, high, plane_forward, depth_forward, depth_backward = lax.optimization_barrier(
        (low, high, plane_forward, depth_forward, depth_backward)
    )
    both, slope, rimmed = call(
        plane_forward_kernel,
        (
            shape((blocks[0], 2 * slabs, width, LANES), bf16),
            shape((slabs, rows, width, cols), f32),
            shape((slabs, (rows + 2) * width, cols), bf16),
        ),
        flops=plane_flops,
    )(slab, low, high, plane_forward, grad_blocks)

    both = lax.all_to_all(both, SPREAD, 0, 0, tiled=True)
    span = (peers + 6) * width
    back_pencil, depth_term = call(
        functools.partial(depth_kernel, lax.axis_size("wide_2"), group_size(SPREAD[1:])),
        (shape(blocks, bf16), shape((width, 8 * width), f32)),
        (
            pltpu.VMEM((span, slabs * LANES), bf16),
            pltpu.VMEM((span, slabs * LANES), bf16),
            pltpu.VMEM((2 * width, 8 * width), f32),
        ),
        flops=3 * depth_flops,
    )(both, depth_forward, depth_backward)
    back = lax.all_to_all(back_pencil, SPREAD, 0, 0, tiled=True)

    pre_grad, packed = call(
        plane_grad_kernel,
        (shape((rows, slabs, width, cols), bf16), shape((8, width, 2 * width), f32)),
        (pltpu.VMEM((3 * width, 3 * width), f32),),
        flops=plane_flops,
    )(back, slope, rimmed, depth_term)
    low = from_below(pre_grad[rows - 1], "narrow")
    high = from_above(pre_grad[0], "narrow")
    pieces = spread_pieces(packed)
    pieces = lax.all_to_all(copies_of(pieces, group_size(TALL)), TALL, 0, 0, tiled=True)
    pieces, plane_backward = lax.optimization_barrier((pieces, plane_backward))
    (volume_grad,) = call(
        plane_backward_kernel,
        (shape((rows, slabs, width, cols), bf16),),
        (pltpu.VMEM((slabs, (rows + 2) * width, cols), bf16),),
        flops=plane_flops,
    )(pre_grad, low, high, grad_blocks, plane_backward)
    volume_grad = volume_grad.transpose(2, 1, 0, 3)
    total = lax.all_to_all(copies_of(pieces, group_size(FLAT)), FLAT, 0, 0, tiled=True)
    plane_total, depth_total = call(
        functools.partial(unpack_kernel, gradient_scale),
        (shape((9, width, width), f32), shape((7, width, width), f32)),
    )(total.reshape(packed.shape))
    return volume_grad, plane_total, depth_total


def solution(mesh):
    names = WIDE + ("narrow",)
    finer = Mesh(mesh.devices.reshape(*FACTORS, mesh.shape["narrow"]), names)
    return jax.shard_map(
        on_device,
        mesh=finer,
        in_specs=(P(None, WIDE, "narrow", None), P(None, WIDE, "narrow", None), P(), P()),
        out_specs=(P(None, WIDE, "narrow", None), P(), P()),
        check_vma=False,
    )
```
